32 devices in a mesh: row: 2 (over core), col: 16 (over z, y, x).
Axes of the slice: x: 2, y: 2, z: 4, core: 2. Of those that a mesh axis runs over, the one named last changes fastest.
Arguments:
- node_feats: bfloat16 [256, 25, 128], P(('row', 'col')), may hold values from -6 to 6
- grad_out: bfloat16 [256, 25, 128], P(('row', 'col')), may hold values from -6 to 6
- edge_src: int32 [2, 16, 512], P('row', 'col'), may hold values from 0 to 15
- edge_tgt: int32 [2, 16, 512], P('row', 'col'), may hold values from 0 to 127
- edge_counts: int32 [2, 16], P('row', 'col'), may hold values from 64 to 512, as said below
- wigner: bfloat16 [2, 16, 512, 475], P('row', 'col'), may hold values from -1 to 1, as said below
- w_zero: bfloat16 [1280, 640], replicated, may hold values from -0.15625 to 0.15625
- w_one: bfloat16 [2, 1024, 512], replicated, may hold values from -0.1875 to 0.1875
- w_two: bfloat16 [2, 768, 384], replicated, may hold values from -0.21875 to 0.21875
Outputs:
- grad_nodes: float32 [256, 25, 128], P(('row', 'col'))
The draws below stay inside these ranges and needn't reach their ends.
Inputs may be any that keep to these rules, and one draw needn't show every extreme that they name: `edge_counts`: slots at or past a tile's count are ignored. In every row of tiles one tile holds exactly 512 edges. `edge_src`: slot values at or past the tile's count are arbitrary but in range. `edge_tgt`: slot values at or past the tile's count are arbitrary but in range. `wigner`: for every degree l, the rows of orders -2..2 (as far as l allows) hold the matching rows of an orthogonal (2l+1) x (2l+1) block in the columns of degree l, column index l*l + l + m; all other entries are zero.
All inputs are finite; a program needn't handle non-finite values.
Results may differ from the reference program's by a relative error of at most 0.015.
Values may be sent and summed in bfloat16 or wider, within the bound.
No kernel may reach another device: no remote copies, remote signals or barrier semaphores. Data moves between devices by JAX's collectives and lax.ppermute only.
A program may use at most 64 MiB of HBM per device.

```python
import jax
import jax.numpy as jnp
from jax import lax

A_DEV = 8
E_CAP = 512
C = 128
COEF = 25
ROW_TILES = 2
COL_TILES = 16
TGT_TILE = 128
SRC_TILE = 16
ATOMS = 256


rotated_order = ((0, 0), (1, 0), (2, 0), (3, 0), (4, 0), (1, 1), (2, 1), (3, 1), (4, 1), (1, -1), (2, -1), (3, -1), (4, -1), (2, 2), (3, 2), (4, 2), (2, -2), (3, -2), (4, -2))


def draw_edge_counts(key, part):
    spread = jax.random.randint(jax.random.fold_in(key, 1), (ROW_TILES, COL_TILES), E_CAP // 8, 3 * E_CAP // 4 + 1)
    full_column = jax.random.randint(jax.random.fold_in(key, 2), (ROW_TILES, 1), 0, COL_TILES)
    columns = jnp.arange(COL_TILES, dtype=jnp.int32)[None, :]
    return jnp.where(columns == full_column, E_CAP, spread).astype(jnp.int32)


def draw_wigner(key, part):
    leading = (ROW_TILES, COL_TILES, E_CAP)
    blocks = []
    for degree in range(5):
        block_width = 2 * degree + 1
        normal_block = jax.random.normal(jax.random.fold_in(key, 10 + degree), leading + (block_width, block_width), jnp.float32)
        orthogonal, triangle = jnp.linalg.qr(normal_block)
        blocks.append(orthogonal)
    rows_out = []
    for degree, order_m in rotated_order:
        block_width = 2 * degree + 1
        picked = blocks[degree][..., degree + order_m, :]
        before = jnp.zeros(leading + (degree * degree,), jnp.float32)
        behind = jnp.zeros(leading + (25 - degree * degree - block_width,), jnp.float32)
        rows_out.append(jnp.concatenate([before, picked, behind], axis=-1))
    return jnp.stack(rows_out, axis=-2).reshape(leading + (475,)).astype(jnp.bfloat16)


def with_ends(entries, key, low, top_value):
    shape = entries.shape
    index_at = [jax.random.randint(jax.random.fold_in(key, axis), (), 0, shape[axis]) for axis in range(len(shape))]
    entries = entries.at[tuple(index_at)].set(low)
    longest = shape.index(max(shape))
    index_at[longest] = (index_at[longest] + 1) % shape[longest]
    return entries.at[tuple(index_at)].set(top_value)


def block_scale(stream_key, extent, pieces, smallest, high):
    level = 1.0
    for axis_at, blocks in pieces:
        heights = jax.random.uniform(jax.random.fold_in(jax.random.fold_in(stream_key, 6), axis_at), (blocks,), jnp.float32, smallest / len(pieces), high / len(pieces))
        level = level * jnp.repeat(jnp.exp(heights), extent[axis_at] // blocks).reshape((-1,) + (1,) * (len(extent) - 1 - axis_at))
    return level


def normal_values(key, extent, width, reach, shards=(), kind=jnp.bfloat16):
    drawn = jax.random.normal(key, extent, jnp.float32) * width
    if len(shards) > 0:
        drawn = block_scale(key, extent, shards, -0.22, 0.18) * drawn
    return jnp.clip(drawn, min=-reach, max=reach).astype(kind)


def setup_inputs(seed: int = 0) -> dict:
    keys = jax.random.split(jax.random.key(seed), 10)
    return {
        "node_feats": normal_values(keys[0], (ATOMS, COEF, C), 1.0, 6.0, ((0, 32),)),
        "grad_out": normal_values(keys[1], (ATOMS, COEF, C), 1.0, 6.0, ((0, 32),)),
        "edge_src": with_ends(jax.random.randint(keys[2], (ROW_TILES, COL_TILES, E_CAP), 0, SRC_TILE), jax.random.fold_in(keys[2], 1), 0, SRC_TILE - 1).astype(jnp.int32),
        "edge_tgt": with_ends(jax.random.randint(keys[3], (ROW_TILES, COL_TILES, E_CAP), 0, TGT_TILE), jax.random.fold_in(keys[3], 1), 0, TGT_TILE - 1).astype(jnp.int32),
        "edge_counts": draw_edge_counts(jax.random.fold_in(keys[9], 71), 0),
        "wigner": draw_wigner(jax.random.fold_in(keys[9], 71), 0),
        "w_zero": normal_values(keys[6], (10 * C, 5 * C), (10 * C) ** -0.5, 0.15625),
        "w_one": normal_values(keys[7], (2, 8 * C, 4 * C), (8 * C) ** -0.5, 0.1875),
        "w_two": normal_values(keys[8], (2, 6 * C, 3 * C), (6 * C) ** -0.5, 0.21875),
    }


def so2_apply(edge_in, w_zero, w_one, w_two):
    edge_count = edge_in.shape[0]
    zero_part = jnp.dot(edge_in[:, 0:5].reshape(edge_count, -1).astype(jnp.float32), w_zero.astype(jnp.float32), preferred_element_type=jnp.float32)
    outputs = [zero_part.reshape(edge_count, 5, -1)]
    for first_row, row_count, weights in ((5, 4, w_one), (13, 3, w_two)):
        plus_part = edge_in[:, first_row:first_row + row_count].reshape(edge_count, -1)
        minus_part = edge_in[:, first_row + row_count:first_row + 2 * row_count].reshape(edge_count, -1)
        stacked = jnp.concatenate([plus_part, minus_part], axis=0)
        real_out = jnp.dot(stacked.astype(jnp.float32), weights[0].astype(jnp.float32), preferred_element_type=jnp.float32)
        imag_out = jnp.dot(stacked.astype(jnp.float32), weights[1].astype(jnp.float32), preferred_element_type=jnp.float32)
        outputs.append((real_out[:edge_count] - imag_out[edge_count:]).reshape(edge_count, row_count, -1))
        outputs.append((real_out[edge_count:] + imag_out[:edge_count]).reshape(edge_count, row_count, -1))
    return jnp.concatenate(outputs, axis=1)

def so2_transpose(grad_y, w_zero, w_one, w_two):
    edge_count = grad_y.shape[0]
    zero_part = jnp.dot(grad_y[:, 0:5].reshape(edge_count, -1).astype(jnp.float32), w_zero.T.astype(jnp.float32), preferred_element_type=jnp.float32)
    outputs = [zero_part.reshape(edge_count, 5, -1)]
    for first_row, row_count, weights in ((5, 4, w_one), (13, 3, w_two)):
        plus_grad = grad_y[:, first_row:first_row + row_count].reshape(edge_count, -1)
        minus_grad = grad_y[:, first_row + row_count:first_row + 2 * row_count].reshape(edge_count, -1)
        stacked = jnp.concatenate([plus_grad, minus_grad], axis=0)
        real_back = jnp.dot(stacked.astype(jnp.float32), weights[0].T.astype(jnp.float32), preferred_element_type=jnp.float32)
        imag_back = jnp.dot(stacked.astype(jnp.float32), weights[1].T.astype(jnp.float32), preferred_element_type=jnp.float32)
        outputs.append((real_back[:edge_count] + imag_back[edge_count:]).reshape(edge_count, row_count, -1))
        outputs.append((real_back[edge_count:] - imag_back[:edge_count]).reshape(edge_count, row_count, -1))
    return jnp.concatenate(outputs, axis=1)

def edge_grads(src_feats, tgt_feats, cotangent, rotation, w_zero, w_one, w_two):
    matrix = rotation.astype(jnp.float32)

    def rotate(values):
        return jnp.einsum('ekj,ejc->ekc', matrix, values.astype(jnp.float32))

    def unrotate(values):
        return jnp.einsum('ekj,ekc->ejc', matrix, values.astype(jnp.float32))
    edge_in = jnp.concatenate([rotate(src_feats), rotate(tgt_feats)], axis=2).astype(jnp.bfloat16)
    rotated_cot = rotate(cotangent).astype(jnp.bfloat16)
    output = so2_apply(edge_in, w_zero, w_one, w_two)
    scalar = output[:, 0]
    gating = jax.nn.sigmoid(scalar)
    gate_slope = gating * (1.0 - gating)
    higher = rotated_cot[:, 1:].astype(jnp.float32)
    gate_grad = jnp.sum(higher * output[:, 1:], axis=1)
    first_cot = rotated_cot[:, 0].astype(jnp.float32)
    scalar_grad = first_cot * (gating + scalar * gate_slope) + gate_grad * gate_slope
    grad_y = jnp.concatenate([scalar_grad[:, None], gating[:, None] * higher], axis=1).astype(jnp.bfloat16)
    grad_in = so2_transpose(grad_y, w_zero, w_one, w_two).astype(jnp.bfloat16)
    channels = cotangent.shape[2]
    grad_src = unrotate(grad_in[:, :, :channels]).astype(jnp.bfloat16)
    grad_tgt = unrotate(grad_in[:, :, channels:]).astype(jnp.bfloat16)
    return (grad_src, grad_tgt)

def rounded(values):
    narrow = lax.optimization_barrier(values.astype(jnp.bfloat16))
    return narrow.astype(jnp.float32)

def reference(node_feats, grad_out, edge_src, edge_tgt, edge_counts, wigner, w_zero, w_one, w_two):
    grid_feats = node_feats.reshape(ROW_TILES, COL_TILES, A_DEV, COEF, C)
    grid_cot = grad_out.reshape(ROW_TILES, COL_TILES, A_DEV, COEF, C)
    block_size = min(128, E_CAP)
    target_acc = jnp.zeros((ROW_TILES, TGT_TILE, COEF, C), jnp.float32)
    source_acc = jnp.zeros((COL_TILES, SRC_TILE, COEF, C), jnp.float32)

    def tile_step(totals, tile_index):
        target_acc, source_acc = totals
        row_index = tile_index // COL_TILES
        col_index = tile_index % COL_TILES
        tgt_feats_tile = grid_feats[row_index].reshape(TGT_TILE, COEF, C)
        tgt_cot_tile = grid_cot[row_index].reshape(TGT_TILE, COEF, C)
        src_feats_tile = jnp.take(grid_feats, col_index, axis=1).reshape(SRC_TILE, COEF, C)
        valid_count = edge_counts[row_index, col_index]
        block_count = (valid_count + block_size - 1) // block_size
        src_list = edge_src[row_index, col_index]
        tgt_list = edge_tgt[row_index, col_index]
        rot_list = wigner[row_index, col_index]

        def block_step(block_index, partial_value):
            tgt_part, src_part = partial_value
            start_slot = (block_index * block_size).astype(jnp.int32)
            source_rows = lax.dynamic_slice_in_dim(src_list, start_slot, block_size)
            target_rows = lax.dynamic_slice_in_dim(tgt_list, start_slot, block_size)
            rotation = lax.dynamic_slice_in_dim(rot_list, start_slot, block_size, 0).reshape(block_size, 19, 25)
            in_range = start_slot + jnp.arange(block_size, dtype=jnp.int32) < valid_count
            grad_src, grad_tgt = edge_grads(src_feats_tile[source_rows], tgt_feats_tile[target_rows], tgt_cot_tile[target_rows], rotation, w_zero, w_one, w_two)
            tgt_part = tgt_part.at[target_rows].add(jnp.where(in_range[:, None, None], grad_tgt.astype(jnp.float32), 0.0))
            src_part = src_part.at[source_rows].add(jnp.where(in_range[:, None, None], grad_src.astype(jnp.float32), 0.0))
            return (tgt_part, src_part)
        empty_tgt = jnp.zeros((TGT_TILE, COEF, C), jnp.float32)
        empty_src = jnp.zeros((SRC_TILE, COEF, C), jnp.float32)
        tgt_part, src_part = lax.fori_loop(0, block_count, block_step, (empty_tgt, empty_src))
        target_acc = target_acc.at[row_index].add(rounded(tgt_part))
        source_acc = source_acc.at[col_index].add(rounded(src_part))
        return ((target_acc, source_acc), None)
    totals, unused = lax.scan(tile_step, (target_acc, source_acc), jnp.arange(ROW_TILES * COL_TILES, dtype=jnp.int32))
    target_full = totals[0].reshape(ATOMS, COEF, C)
    source_full = totals[1].reshape(COL_TILES, ROW_TILES, A_DEV, COEF, C).transpose(1, 0, 2, 3, 4).reshape(ATOMS, COEF, C)
    return target_full + source_full
```

```python
import functools

import jax
import jax.numpy as jnp
from jax import lax
from jax.experimental import pallas as pl
from jax.experimental.pallas import tpu as pltpu
from jax.sharding import PartitionSpec as P

C = 128
COEF = 25
ROWS = 19
GROUP = 8
K_PAD = 20 * GROUP
J_PAD = 26 * GROUP
LANES = 256
UNROLL = 4
F32 = jnp.float32
BF16 = jnp.bfloat16


def iota(shape, axis):
    return lax.broadcasted_iota(jnp.int32, shape, axis)


def expand_kernel(wig_ref, fwd_ref, bwd_ref, flat):
    edges = wig_ref.shape[0]
    width = wig_ref.shape[1]
    flat[:, 384:512] = jnp.zeros((edges, 128), BF16)
    flat[:, 0:width] = wig_ref[...]
    same_edge = (iota((edges, LANES), 0) % GROUP) == (iota((edges, LANES), 1) % GROUP)
    source = iota((512, LANES), 0)
    slot = iota((512, LANES), 1) // GROUP

    def picked(wanted):
        chosen = jnp.where(source == wanted, 1.0, 0.0).astype(BF16)
        spread = jnp.dot(flat[...], chosen, preferred_element_type=F32)
        return jnp.where(same_edge, spread, 0.0).reshape(edges // GROUP, GROUP, LANES)

    def fwd_step(pair, unused):
        parts = []
        for odd in range(2):
            k = pair * 2 + odd
            wanted = jnp.where((slot < COEF) & (k < ROWS), k * COEF + slot, -1)
            parts.append(picked(wanted))
        start = pl.multiple_of(pair * 16, 16)
        fwd_ref[:, pl.ds(start, 16), :] = jnp.concatenate(parts, axis=1).astype(BF16)
        return unused

    def bwd_step(pair, unused):
        parts = []
        for odd in range(2):
            j = pair * 2 + odd
            wanted = jnp.where((slot < ROWS) & (j < COEF), slot * COEF + j, -1)
            parts.append(picked(wanted))
        start = pl.multiple_of(pair * 16, 16)
        bwd_ref[:, pl.ds(start, 16), :] = jnp.concatenate(parts, axis=1).astype(BF16)
        return unused

    lax.fori_loop(0, K_PAD // 16, fwd_step, 0)
    lax.fori_loop(0, J_PAD // 16, bwd_step, 0)


def gather_atoms(ids_ref, feats_ref, table, gathered):
    blocks = feats_ref.shape[0]
    edges = ids_ref.shape[0]
    for j in range(COEF):
        column = jnp.concatenate([feats_ref[b, j].astype(F32) for b in range(blocks)], axis=0)
        table[:, j * C : (j + 1) * C] = column.astype(BF16)
    atoms = blocks * 8
    hot = jnp.where(ids_ref[...] == iota((edges, atoms), 1), 1.0, 0.0).astype(BF16)
    for j in range(0, COEF, 5):
        gathered[:, j * C : (j + 5) * C] = jnp.dot(
            hot, table[:, j * C : (j + 5) * C], preferred_element_type=F32
        )


def rotate_group(rot_ref, gathered, g):
    start = pl.multiple_of(g * GROUP, GROUP)
    rows = [gathered[pl.ds(start, GROUP), j * C : (j + 1) * C] for j in range(COEF)]
    rows.append(jnp.zeros((LANES - COEF * GROUP, C), F32))
    right = jnp.concatenate(rows, axis=0).astype(BF16)
    return jnp.dot(rot_ref[g], right, preferred_element_type=F32)


def pair_row(first, second, k):
    return jnp.concatenate([first[k * 8 : k * 8 + 8], second[k * 8 : k * 8 + 8]], axis=0)


def forward_kernel(has_prev, *refs):
    ids_ref, feats_ref, rot_ref, w0_ref, w1_ref, w2_ref = refs[:6]
    refs = refs[6:]
    if has_prev:
        prev, refs = refs[:3], refs[3:]
    outs = refs[:3]
    table, gathered, l0, l1, l2 = refs[3:]
    edges = ids_ref.shape[0]
    gather_atoms(ids_ref, feats_ref, table, gathered)

    def step(i, unused):
        for u in range(0, UNROLL, 2):
            g = i * UNROLL + u
            first = rotate_group(rot_ref, gathered, g)
            second = rotate_group(rot_ref, gathered, g + 1)
            top = pl.ds(pl.multiple_of(g * GROUP, 16), 16)
            low = pl.ds(pl.multiple_of(g * GROUP + edges, 16), 16)
            for k in range(5):
                l0[top, k * C : (k + 1) * C] = pair_row(first, second, k).astype(BF16)
            for left, base, count in ((l1, 5, 4), (l2, 13, 3)):
                half = count * C
                for n in range(count):
                    p = pair_row(first, second, base + n)
                    q = pair_row(first, second, base + count + n)
                    here = slice(n * C, (n + 1) * C)
                    there = slice(half + n * C, half + (n + 1) * C)
                    left[top, here] = p.astype(BF16)
                    left[top, there] = (-q).astype(BF16)
                    left[low, here] = q.astype(BF16)
                    left[low, there] = p.astype(BF16)
        return unused

    lax.fori_loop(0, edges // (GROUP * UNROLL), step, 0)
    for n, (left, w_ref) in enumerate(((l0, w0_ref), (l1, w1_ref), (l2, w2_ref))):
        width = w_ref.shape[-1]
        weight = w_ref[...].reshape(-1, width)
        value = jnp.dot(left[...], weight, preferred_element_type=F32)
        if has_prev:
            value = value + prev[n][...]
        outs[n][...] = value


def y_slices(edges, start):
    out = []
    for k in range(5):
        out.append((0, start, k))
    for base, count in ((1, 4), (2, 3)):
        for sign in range(2):
            for n in range(count):
                out.append((base, start + sign * edges, n))
    return out


def back_half(lefts, w_refs, rot_ref, grad_in, edge_grad):
    edges = lefts[0].shape[0]
    dims = (((1,), (1,)), ((), ()))
    for n in range(3):
        w_ref = w_refs[n]
        width = w_ref.shape[-1]
        if n == 0:
            weight = w_ref[...].reshape(-1, width)
            grad_in[0][...] = lax.dot_general(
                lefts[0][...], weight, dims, preferred_element_type=F32
            )
        else:
            real = w_ref[0].reshape(-1, width)
            imag = w_ref[1].reshape(-1, width)
            grad_in[n][...] = lax.dot_general(
                lefts[n][:, :width], real, dims, preferred_element_type=F32
            ) + lax.dot_general(lefts[n][:, width:], imag, dims, preferred_element_type=F32)

    def one(g):
        start = pl.multiple_of(g * GROUP, GROUP)
        rows = []
        for which, row, n in y_slices(edges, start):
            rows.append(
                grad_in[which][pl.ds(pl.multiple_of(row, GROUP), GROUP), n * C : (n + 1) * C]
            )
        rows.append(jnp.zeros((LANES - ROWS * GROUP, C), F32))
        right = jnp.concatenate(rows, axis=0).astype(BF16)
        return jnp.dot(rot_ref[g], right, preferred_element_type=F32)

    def step(i, unused):
        for u in range(0, UNROLL, 2):
            g = i * UNROLL + u
            first, second = one(g), one(g + 1)
            top = pl.ds(pl.multiple_of(g * GROUP, 16), 16)
            for j in range(COEF):
                edge_grad[top, j * C : (j + 1) * C] = pair_row(first, second, j).astype(BF16)
        return unused

    lax.fori_loop(0, edges // (GROUP * UNROLL), step, 0)


def scatter_atoms(ids_row_ref, count_ref, edge_grad, out_ref):
    blocks = out_ref.shape[0]
    atoms = blocks * 8
    edges = edge_grad.shape[0]
    valid = iota((atoms, edges), 1) < count_ref[0]
    hot = jnp.where((ids_row_ref[...] == iota((atoms, edges), 0)) & valid, 1.0, 0.0).astype(BF16)
    for j in range(COEF):
        total = jnp.dot(hot, edge_grad[:, j * C : (j + 1) * C], preferred_element_type=F32)
        for b in range(blocks):
            out_ref[b, j] = total[b * 8 : b * 8 + 8].astype(out_ref.dtype)


def target_back_kernel(*refs):
    ids_ref, row_ref, count_ref, cot_ref, fwd_ref, bwd_ref = refs[:6]
    w_refs, ys, lefts = refs[6:9], refs[9:12], refs[12:15]
    out_ref = refs[15]
    table, gathered, g0, g1, g2, edge_grad = refs[16:]
    edges = ids_ref.shape[0]
    gather_atoms(ids_ref, cot_ref, table, gathered)

    def step(i, unused):
        for u in range(0, UNROLL, 2):
            g = i * UNROLL + u
            first = rotate_group(fwd_ref, gathered, g)
            second = rotate_group(fwd_ref, gathered, g + 1)
            start = g * GROUP
            top = pl.ds(pl.multiple_of(start, 16), 16)
            low = pl.ds(pl.multiple_of(start + edges, 16), 16)
            cots = [pair_row(first, second, k).astype(BF16).astype(F32) for k in range(ROWS)]
            where = y_slices(edges, start)

            def y_at(k):
                which, row, n = where[k]
                return ys[which][pl.ds(pl.multiple_of(row, 16), 16), n * C : (n + 1) * C]

            y0 = y_at(0)
            gating = jax.nn.sigmoid(y0)
            slope = gating * (1.0 - gating)
            total = cots[1] * y_at(1)
            for k in range(2, ROWS):
                total = total + cots[k] * y_at(k)
            scalar = cots[0] * (gating + y0 * slope) + total * slope
            grads = [scalar] + [gating * cots[k] for k in range(1, ROWS)]
            for k in range(5):
                lefts[0][top, k * C : (k + 1) * C] = grads[k].astype(BF16)
            for n, base, count in ((1, 5, 4), (2, 13, 3)):
                left = lefts[n]
                half = count * C
                for m in range(count):
                    a = grads[base + m]
                    b = grads[base + count + m]
                    here = slice(m * C, (m + 1) * C)
                    there = slice(half + m * C, half + (m + 1) * C)
                    left[top, here] = a.astype(BF16)
                    left[top, there] = b.astype(BF16)
                    left[low, here] = b.astype(BF16)
                    left[low, there] = (-a).astype(BF16)
        return unused

    lax.fori_loop(0, edges // (GROUP * UNROLL), step, 0)
    back_half(lefts, w_refs, bwd_ref, (g0, g1, g2), edge_grad)
    scatter_atoms(row_ref, count_ref, edge_grad, out_ref)


def source_back_kernel(*refs):
    row_ref, count_ref, bwd_ref = refs[:3]
    w_refs, lefts, out_ref = refs[3:6], refs[6:9], refs[9]
    g0, g1, g2, edge_grad = refs[10:]
    back_half(lefts, w_refs, bwd_ref, (g0, g1, g2), edge_grad)
    scatter_atoms(row_ref, count_ref, edge_grad, out_ref)


VMEM_LIMIT = 56 * 1024 * 1024


def whole(shape):
    return pl.BlockSpec(shape, lambda i: (0,) * len(shape))


def half_specs(half):
    return [
        pl.BlockSpec((5, 1, C, 5 * C), lambda i: (0, half, 0, 0)),
        pl.BlockSpec((2, 4, 1, C, 4 * C), lambda i: (0, 0, half, 0, 0)),
        pl.BlockSpec((2, 3, 1, C, 3 * C), lambda i: (0, 0, half, 0, 0)),
    ]


def call(kernel, args, specs, outs, scratch, flops, aliases=None):
    moved = sum(a.size * a.dtype.itemsize for a in args) + sum(
        o.size * o.dtype.itemsize for o in outs
    )
    return pl.pallas_call(
        kernel,
        grid=(1,),
        in_specs=specs,
        out_specs=[whole(o.shape) for o in outs],
        out_shape=outs,
        scratch_shapes=scratch,
        input_output_aliases=aliases or {},
        compiler_params=pltpu.CompilerParams(vmem_limit_bytes=VMEM_LIMIT),
        cost_estimate=pl.CostEstimate(flops=flops, bytes_accessed=moved, transcendentals=0),
    )(*args)


def expand(wig):
    edges = wig.shape[0]
    groups = edges // GROUP
    outs = [
        jax.ShapeDtypeStruct((groups, K_PAD, LANES), BF16),
        jax.ShapeDtypeStruct((groups, J_PAD, LANES), BF16),
    ]
    return call(
        expand_kernel,
        [wig],
        [whole(wig.shape)],
        outs,
        [pltpu.VMEM((edges, 512), BF16)],
        2 * 46 * edges * 512 * 256,
    )


def y_shapes(edges):
    return [
        jax.ShapeDtypeStruct((edges, 5 * C), F32),
        jax.ShapeDtypeStruct((2 * edges, 4 * C), F32),
        jax.ShapeDtypeStruct((2 * edges, 3 * C), F32),
    ]


def left_shapes(edges):
    return [(edges, 5 * C), (2 * edges, 8 * C), (2 * edges, 6 * C)]


def forward(half, ids, feats, rot, weights, prev):
    edges = ids.shape[0]
    atoms = feats.shape[0] * 8
    args = [ids, feats, rot, *weights]
    specs = [whole(ids.shape), whole(feats.shape), whole(rot.shape), *half_specs(half)]
    outs = y_shapes(edges)
    aliases = None
    if prev is not None:
        aliases = {len(args) + n: n for n in range(3)}
        args += prev
        specs += [whole(o.shape) for o in outs]
    scratch = [pltpu.VMEM((atoms, COEF * C), BF16), pltpu.VMEM((edges, COEF * C), F32)]
    scratch += [pltpu.VMEM(s, BF16) for s in left_shapes(edges)]
    kernel = functools.partial(forward_kernel, prev is not None)
    return call(kernel, args, specs, outs, scratch, 2 * edges * 65536 * 64, aliases)


def target_back(ids, row, count, cot, fwd, bwd, weights, ys):
    edges = ids.shape[0]
    blocks = cot.shape[0]
    args = [ids, row, count, cot, fwd, bwd, *weights, *ys]
    specs = [whole(ids.shape), whole(row.shape), pl.BlockSpec(memory_space=pltpu.SMEM)]
    specs += [whole(cot.shape), whole(fwd.shape), whole(bwd.shape), *half_specs(1)]
    specs += [whole(y.shape) for y in ys]
    outs = [jax.ShapeDtypeStruct(s, BF16) for s in left_shapes(edges)]
    outs.append(jax.ShapeDtypeStruct((blocks, COEF, 8, C), BF16))
    scratch = [pltpu.VMEM((blocks * 8, COEF * C), BF16), pltpu.VMEM((edges, COEF * C), F32)]
    scratch += [pltpu.VMEM(o.shape, F32) for o in y_shapes(edges)]
    scratch.append(pltpu.VMEM((edges, COEF * C), BF16))
    return call(target_back_kernel, args, specs, outs, scratch, 2 * edges * 65536 * 95)


def source_back(row, count, bwd, weights, lefts, blocks):
    edges = lefts[0].shape[0]
    args = [row, count, bwd, *weights, *lefts]
    specs = [whole(row.shape), pl.BlockSpec(memory_space=pltpu.SMEM), whole(bwd.shape)]
    specs += half_specs(0) + [whole(v.shape) for v in lefts]
    outs = [jax.ShapeDtypeStruct((blocks, COEF, 8, C), BF16)]
    scratch = [pltpu.VMEM(o.shape, F32) for o in y_shapes(edges)]
    scratch.append(pltpu.VMEM((edges, COEF * C), BF16))
    return call(source_back_kernel, args, specs, outs, scratch, 2 * edges * 65536 * 70)[0]


def spread(block, axis):
    size = lax.axis_size(axis)
    return lax.all_to_all(jnp.broadcast_to(block[None], (size, *block.shape)), axis, 0, 0)


def local(node_feats, grad_out, edge_src, edge_tgt, edge_counts, wigner, w_zero, w_one, w_two):
    feats = node_feats.transpose(1, 0, 2)
    cot = grad_out.transpose(1, 0, 2)
    source_feats = lax.all_gather(feats, "row", axis=0)
    target_feats = spread(feats, "col")
    target_cot = spread(cot, "col")
    weights = (
        w_zero.reshape(5, 2, C, 5 * C),
        w_one.reshape(2, 4, 2, C, 4 * C),
        w_two.reshape(2, 3, 2, C, 3 * C),
    )
    count = edge_counts.reshape(1)
    edges = edge_src.shape[-1]
    src_col, tgt_col = edge_src.reshape(edges, 1), edge_tgt.reshape(edges, 1)
    src_row, tgt_row = edge_src.reshape(1, edges), edge_tgt.reshape(1, edges)
    fwd, bwd = expand(wigner[0, 0])
    ys = forward(0, src_col, source_feats, fwd, weights, None)
    ys = forward(1, tgt_col, target_feats, fwd, weights, list(ys))
    *lefts, tile_tgt = target_back(
        tgt_col, tgt_row, count, target_cot, fwd, bwd, weights, list(ys)
    )
    tile_src = source_back(src_row, count, bwd, weights, lefts, source_feats.shape[0])
    own = lax.all_to_all(tile_tgt, "col", 0, 0).astype(F32).sum(0)
    cross = lax.all_to_all(tile_src, "row", 0, 0).astype(F32).sum(0)
    return (own + cross).transpose(1, 0, 2)


def solution(mesh):
    placed = (
        P(("row", "col"), None, None),
        P(("row", "col"), None, None),
        P("row", "col", None),
        P("row", "col", None),
        P("row", "col"),
        P("row", "col", None, None),
        P(),
        P(),
        P(),
    )
    return jax.shard_map(
        local, mesh=mesh, in_specs=placed, out_specs=P(("row", "col"), None, None), check_vma=False
    )
```

```python
import functools

import jax
import jax.numpy as jnp
from jax import lax
from jax.experimental import pallas as pl
from jax.experimental.pallas import tpu as pltpu
from jax.sharding import PartitionSpec as P


C = 128
COEF = 25
ROWS = 19
GROUP = 8
K_PAD = 20 * GROUP
J_PAD = 26 * GROUP
LANES = 256
CHUNK = 256
UNROLL = 4
F32 = jnp.float32
BF16 = jnp.bfloat16
MIB = 1024 * 1024
NT = (((1,), (1,)), ((), ()))


def iota(shape, axis):
    return lax.broadcasted_iota(jnp.int32, shape, axis)


def expand_kernel(wig_ref, fwd_ref, bwd_ref, flat):
    edges = wig_ref.shape[0]
    width = wig_ref.shape[1]
    flat[:, 384:512] = jnp.zeros((edges, 128), BF16)
    flat[:, 0:width] = wig_ref[...]
    same_edge = (iota((edges, LANES), 0) % GROUP) == (iota((edges, LANES), 1) % GROUP)
    source = iota((512, LANES), 0)
    slot = iota((512, LANES), 1) // GROUP

    def picked(wanted):
        chosen = jnp.where(source == wanted, 1.0, 0.0).astype(BF16)
        spread = jnp.dot(flat[...], chosen, preferred_element_type=F32)
        return jnp.where(same_edge, spread, 0.0).reshape(edges // GROUP, GROUP, LANES)

    def fwd_step(pair, unused):
        parts = []
        for odd in range(2):
            k = pair * 2 + odd
            wanted = jnp.where((slot < COEF) & (k < ROWS), k * COEF + slot, -1)
            parts.append(picked(wanted))
        start = pl.multiple_of(pair * 16, 16)
        fwd_ref[:, pl.ds(start, 16), :] = jnp.concatenate(parts, axis=1).astype(BF16)
        return unused

    def bwd_step(pair, unused):
        parts = []
        for odd in range(2):
            j = pair * 2 + odd
            wanted = jnp.where((slot < ROWS) & (j < COEF), slot * COEF + j, -1)
            parts.append(picked(wanted))
        start = pl.multiple_of(pair * 16, 16)
        bwd_ref[:, pl.ds(start, 16), :] = jnp.concatenate(parts, axis=1).astype(BF16)
        return unused

    lax.fori_loop(0, K_PAD // 16, fwd_step, 0)
    lax.fori_loop(0, J_PAD // 16, bwd_step, 0)


def aligned(value, by):
    return pl.multiple_of(value, by)


def fill_table(blocks, table, kinds):
    width = kinds * C
    for j in range(COEF):
        for kind in range(kinds):
            column = jnp.concatenate([block(kind, j).astype(F32) for block in blocks], axis=0)
            start = j * width + kind * C
            table[:, start : start + C] = column.astype(BF16)


def source_hot(ids_ref, chunk, atoms):
    ids = ids_ref[:, pl.ds(aligned(chunk * CHUNK, CHUNK), CHUNK)]
    place = ids ^ (lax.axis_index("row") * 8)
    return place == iota((atoms, CHUNK), 0)


def target_hot(ids_ref, chunk, atoms, inner):
    ids = ids_ref[:, pl.ds(aligned(chunk * CHUNK, CHUNK), CHUNK)]
    place = ids ^ (lax.axis_index("col") * 8)
    block = place // 8
    outer = atoms // (8 * inner)
    place = ((block % inner) * outer + block // inner) * 8 + place % 8
    return place == iota((atoms, CHUNK), 0)


def gather_atoms(hot, table, gathered):
    hot = jnp.where(hot, 1.0, 0.0).T.astype(BF16)
    step = gathered.shape[1] // 5
    for n in range(5):
        gathered[:, n * step : (n + 1) * step] = jnp.dot(
            hot, table[:, n * step : (n + 1) * step], preferred_element_type=F32
        )


def rotate_group(rot_ref, g, gathered, local_g):
    width = gathered.shape[1] // COEF
    start = aligned(local_g * GROUP, GROUP)
    rows = [gathered[pl.ds(start, GROUP), j * width : (j + 1) * width] for j in range(COEF)]
    rows.append(jnp.zeros((LANES - COEF * GROUP, width), F32))
    right = jnp.concatenate(rows, axis=0).astype(BF16)
    return jnp.dot(rot_ref[g], right, preferred_element_type=F32)


def pair_row(first, second, k, kind=0):
    lanes = slice(kind * C, (kind + 1) * C)
    return jnp.concatenate([first[k * 8 : k * 8 + 8, lanes], second[k * 8 : k * 8 + 8, lanes]], 0)


def store_forward(value, lefts, top, low):
    for k in range(5):
        lefts[0][top, k * C : (k + 1) * C] = value(k).astype(BF16)
    for left, base, count in ((lefts[1], 5, 4), (lefts[2], 13, 3)):
        for n in range(count):
            p, q = value(base + n), value(base + count + n)
            here = slice(n * C, (n + 1) * C)
            there = slice((count + n) * C, (count + n + 1) * C)
            left[top, here] = p.astype(BF16)
            left[top, there] = (-q).astype(BF16)
            left[low, here] = q.astype(BF16)
            left[low, there] = p.astype(BF16)


def half_weight(w_ref, n, half):
    width = w_ref.shape[-1]
    if n == 0:
        return w_ref[:, half].reshape(-1, width)
    return w_ref[:, :, half].reshape(-1, width)


def source_forward_kernel(*refs):
    ids_ref, feats_ref, rot_ref = refs[:3]
    w_refs, outs = refs[3:6], refs[6:9]
    table, gathered, lefts = refs[9], refs[10], refs[11:]
    edges = ids_ref.shape[1]
    blocks = [lambda kind, j, b=b: feats_ref[b, j] for b in range(feats_ref.shape[0])]
    fill_table(blocks, table, 1)

    def chunk_step(chunk, unused):
        gather_atoms(source_hot(ids_ref, chunk, table.shape[0]), table, gathered)

        def step(i, unused):
            for u in range(0, UNROLL, 2):
                g = i * UNROLL + u
                pair = [
                    rotate_group(rot_ref, chunk * (CHUNK // GROUP) + g + n, gathered, g + n)
                    for n in range(2)
                ]
                top = pl.ds(aligned(g * GROUP, 16), 16)
                low = pl.ds(aligned(g * GROUP + CHUNK, 16), 16)
                store_forward(lambda k: pair_row(*pair, k), lefts, top, low)
            return unused

        lax.fori_loop(0, CHUNK // (GROUP * UNROLL), step, 0)
        for n in range(3):
            rows = lefts[n].shape[0]
            outs[n][pl.ds(aligned(chunk * rows, rows), rows), :] = jnp.dot(
                lefts[n][...], half_weight(w_refs[n], n, 0), preferred_element_type=F32
            )
        return unused

    lax.fori_loop(0, edges // CHUNK, chunk_step, 0)


def y_slices(start):
    out = [(0, start, k) for k in range(5)]
    for which, count in ((1, 4), (2, 3)):
        for sign in range(2):
            out += [(which, start + sign * CHUNK, n) for n in range(count)]
    return out


def back_half(half, chunk, lefts, w_refs, rot_ref, grad_in, edge_grad):
    for n in range(3):
        width = w_refs[n].shape[-1]
        rows = grad_in[n].shape[0]
        here = pl.ds(aligned(chunk * rows, rows), rows)
        if n == 0:
            weight = w_refs[n][:, half].reshape(-1, width)
            grad_in[n][...] = lax.dot_general(
                lefts[n][here, :], weight, NT, preferred_element_type=F32
            )
        else:
            real = w_refs[n][0, :, half].reshape(-1, width)
            imag = w_refs[n][1, :, half].reshape(-1, width)
            grad_in[n][...] = lax.dot_general(
                lefts[n][here, :width], real, NT, preferred_element_type=F32
            ) + lax.dot_general(lefts[n][here, width:], imag, NT, preferred_element_type=F32)

    def one(g):
        rows = []
        for which, row, n in y_slices(g * GROUP):
            rows.append(grad_in[which][pl.ds(aligned(row, GROUP), GROUP), n * C : (n + 1) * C])
        rows.append(jnp.zeros((LANES - ROWS * GROUP, C), F32))
        right = jnp.concatenate(rows, axis=0).astype(BF16)
        return jnp.dot(
            rot_ref[chunk * (CHUNK // GROUP) + g], right, preferred_element_type=F32
        )

    def step(i, unused):
        for u in range(0, UNROLL, 2):
            g = i * UNROLL + u
            first, second = one(g), one(g + 1)
            top = pl.ds(aligned(g * GROUP, 16), 16)
            for j in range(COEF):
                edge_grad[top, j * C : (j + 1) * C] = pair_row(first, second, j).astype(BF16)
        return unused

    lax.fori_loop(0, CHUNK // (GROUP * UNROLL), step, 0)


def scatter_atoms(hot, count_ref, chunk, edge_grad, total):
    valid = chunk * CHUNK + iota(hot.shape, 1) < count_ref[0, 0]
    hot = jnp.where(hot & valid, 1.0, 0.0).astype(BF16)
    step = total.shape[1] // 5
    for n in range(5):
        here = slice(n * step, (n + 1) * step)
        total[:, here] += jnp.dot(hot, edge_grad[:, here], preferred_element_type=F32)


def write_blocks(total, out_ref):
    for j in range(COEF):
        for b in range(out_ref.shape[0]):
            out_ref[b, j] = total[b * 8 : b * 8 + 8, j * C : (j + 1) * C].astype(out_ref.dtype)


def target_kernel(count_pieces, *refs):
    ids_ref, count_ref, fwd_ref, bwd_ref = refs[:4]
    w_refs, sources = refs[4:7], refs[7:10]
    pieces = refs[10 : 10 + count_pieces]
    refs = refs[10 + count_pieces :]
    lefts, out_ref = refs[:3], refs[3]
    table, gathered = refs[4], refs[5]
    forward_lefts, cots, ys, grad_in = refs[6:9], refs[9], refs[10:13], refs[13:16]
    edge_grad, total = refs[16], refs[17]
    edges = ids_ref.shape[1]
    blocks = []
    for piece in pieces:
        for b in range(piece.shape[0]):
            blocks.append(lambda kind, j, piece=piece, b=b: piece[b, kind, j])
    fill_table(blocks, table, 2)
    total[...] = jnp.zeros_like(total)

    def chunk_step(chunk, unused):
        hot = target_hot(ids_ref, chunk, table.shape[0], count_pieces)
        gather_atoms(hot, table, gathered)

        def turn(i, unused):
            for u in range(0, UNROLL, 2):
                g = i * UNROLL + u
                pair = [
                    rotate_group(fwd_ref, chunk * (CHUNK // GROUP) + g + n, gathered, g + n)
                    for n in range(2)
                ]
                top = pl.ds(aligned(g * GROUP, 16), 16)
                low = pl.ds(aligned(g * GROUP + CHUNK, 16), 16)
                store_forward(lambda k: pair_row(*pair, k), forward_lefts, top, low)
                for k in range(ROWS):
                    cots[top, k * C : (k + 1) * C] = pair_row(*pair, k, 1).astype(BF16)
            return unused

        lax.fori_loop(0, CHUNK // (GROUP * UNROLL), turn, 0)
        for n in range(3):
            rows = forward_lefts[n].shape[0]
            ys[n][...] = sources[n][pl.ds(aligned(chunk * rows, rows), rows), :] + jnp.dot(
                forward_lefts[n][...], half_weight(w_refs[n], n, 1), preferred_element_type=F32
            )

        def gate(i, unused):
            start = aligned(i * 16, 16)
            top = pl.ds(start, 16)
            cot = [cots[top, k * C : (k + 1) * C].astype(F32) for k in range(ROWS)]
            where = y_slices(start)

            def y_at(k):
                which, row, n = where[k]
                return ys[which][pl.ds(aligned(row, 16), 16), n * C : (n + 1) * C]

            y0 = y_at(0)
            gating = jax.nn.sigmoid(y0)
            slope = gating * (1.0 - gating)
            dotted = cot[1] * y_at(1)
            for k in range(2, ROWS):
                dotted = dotted + cot[k] * y_at(k)
            grads = [cot[0] * (gating + y0 * slope) + dotted * slope]
            grads += [gating * cot[k] for k in range(1, ROWS)]
            zero_row = aligned(chunk * CHUNK + start, 16)
            top_row = aligned(chunk * 2 * CHUNK + start, 16)
            low_row = aligned(chunk * 2 * CHUNK + CHUNK + start, 16)
            store_backward(grads, lefts, zero_row, top_row, low_row)
            return unused

        lax.fori_loop(0, CHUNK // 16, gate, 0)
        back_half(1, chunk, lefts, w_refs, bwd_ref, grad_in, edge_grad)
        hot = target_hot(ids_ref, chunk, table.shape[0], count_pieces)
        scatter_atoms(hot, count_ref, chunk, edge_grad, total)
        return unused

    lax.fori_loop(0, edges // CHUNK, chunk_step, 0)
    write_blocks(total, out_ref)


def store_backward(value, lefts, zero_row, top_row, low_row):
    for k in range(5):
        lefts[0][pl.ds(zero_row, 16), k * C : (k + 1) * C] = value[k].astype(BF16)
    top, low = pl.ds(top_row, 16), pl.ds(low_row, 16)
    for left, base, count in ((lefts[1], 5, 4), (lefts[2], 13, 3)):
        for n in range(count):
            a, b = value[base + n], value[base + count + n]
            here = slice(n * C, (n + 1) * C)
            there = slice((count + n) * C, (count + n + 1) * C)
            left[top, here] = a.astype(BF16)
            left[top, there] = b.astype(BF16)
            left[low, here] = b.astype(BF16)
            left[low, there] = (-a).astype(BF16)


def source_back_kernel(*refs):
    ids_ref, count_ref, bwd_ref = refs[:3]
    w_refs, lefts, out_ref = refs[3:6], refs[6:9], refs[9]
    grad_in, edge_grad, total = refs[10:13], refs[13], refs[14]
    total[...] = jnp.zeros_like(total)

    def chunk_step(chunk, unused):
        back_half(0, chunk, lefts, w_refs, bwd_ref, grad_in, edge_grad)
        scatter_atoms(source_hot(ids_ref, chunk, total.shape[0]), count_ref, chunk, edge_grad, total)
        return unused

    lax.fori_loop(0, lefts[0].shape[0] // CHUNK, chunk_step, 0)
    write_blocks(total, out_ref)


IN_VMEM = pl.BlockSpec(memory_space=pltpu.VMEM)
IN_SMEM = pl.BlockSpec(memory_space=pltpu.SMEM)


def call(kernel, args, outs, scratch, limit, flops, scalar=None):
    moved = sum(a.size * a.dtype.itemsize for a in (*args, *outs))
    return pl.pallas_call(
        kernel,
        in_specs=[IN_SMEM if n == scalar else IN_VMEM for n in range(len(args))],
        out_specs=[IN_VMEM] * len(outs),
        out_shape=outs,
        scratch_shapes=[pltpu.VMEM(s, d) for s, d in scratch],
        compiler_params=pltpu.CompilerParams(vmem_limit_bytes=limit * MIB),
        cost_estimate=pl.CostEstimate(flops=flops, bytes_accessed=moved, transcendentals=0),
    )(*args)


def arrays(shapes, dtype):
    return [jax.ShapeDtypeStruct(s, dtype) for s in shapes]


def y_shapes(edges):
    return [(edges, 5 * C), (2 * edges, 4 * C), (2 * edges, 3 * C)]


def left_shapes(edges):
    return [(edges, 5 * C), (2 * edges, 8 * C), (2 * edges, 6 * C)]


def typed(shapes, dtype):
    return [(s, dtype) for s in shapes]


PUSH = 2 * 65536


def expand(wig):
    edges = wig.shape[0]
    groups = edges // GROUP
    outs = arrays([(groups, K_PAD, LANES), (groups, J_PAD, LANES)], BF16)
    scratch = [((edges, 512), BF16)]
    return call(expand_kernel, [wig], outs, scratch, 12, PUSH * edges * 92)


def source_forward(ids, feats, rot, weights):
    edges = ids.shape[1]
    scratch = [((feats.shape[0] * 8, COEF * C), BF16), ((CHUNK, COEF * C), F32)]
    scratch += typed(left_shapes(CHUNK), BF16)
    return call(
        source_forward_kernel,
        [ids, feats, rot, *weights],
        arrays(y_shapes(edges), F32),
        scratch,
        12,
        PUSH * edges * 64,
    )


def target_work(ids, count, fwd, bwd, weights, sources, pieces):
    edges = ids.shape[1]
    blocks = sum(p.shape[0] for p in pieces)
    outs = arrays(left_shapes(edges), BF16) + arrays([(blocks, COEF, 8, C)], BF16)
    scratch = [((blocks * 8, 2 * COEF * C), BF16), ((CHUNK, 2 * COEF * C), F32)]
    scratch += typed(left_shapes(CHUNK), BF16) + [((CHUNK, ROWS * C), BF16)]
    scratch += typed(y_shapes(CHUNK), F32) * 2
    scratch += [((CHUNK, COEF * C), BF16), ((blocks * 8, COEF * C), F32)]
    return call(
        functools.partial(target_kernel, len(pieces)),
        [ids, count, fwd, bwd, *weights, *sources, *pieces],
        outs,
        scratch,
        21 + blocks // 4,
        PUSH * edges * 160,
        1,
    )


def source_back(ids, count, bwd, weights, lefts, blocks):
    scratch = typed(y_shapes(CHUNK), F32)
    scratch += [((CHUNK, COEF * C), BF16), ((blocks * 8, COEF * C), F32)]
    return call(
        source_back_kernel,
        [ids, count, bwd, *weights, *lefts],
        arrays([(blocks, COEF, 8, C)], BF16),
        scratch,
        12,
        PUSH * lefts[0].shape[0] * 70,
        1,
    )[0]


def exchange(value, axis, distance):
    size = lax.axis_size(axis)
    return lax.ppermute(value, axis, [(i, i ^ distance) for i in range(size)])


def step(node_feats, grad_out, edge_src, edge_tgt, count, wigner, w_zero, w_one, w_two):
    rows, cols = lax.axis_size("row"), lax.axis_size("col")
    inner = 4
    outer = cols // inner
    feats = node_feats.transpose(1, 0, 2)
    own = jnp.stack([feats, grad_out.transpose(1, 0, 2)])
    source_feats = [feats] + [exchange(feats, "row", d) for d in range(1, rows)]
    source_feats = jnp.stack(source_feats)
    line = [own]
    for d in range(1, outer):
        line.append(exchange(own, "col", inner * d))
    line = jnp.stack(line)
    pieces = [line]
    for d in range(1, inner):
        pieces.append(exchange(line, "col", d))

    weights = (
        w_zero.reshape(5, 2, C, 5 * C),
        w_one.reshape(2, 4, 2, C, 4 * C),
        w_two.reshape(2, 3, 2, C, 3 * C),
    )
    edges = edge_src.shape[-1]
    src, tgt = edge_src.reshape(1, edges), edge_tgt.reshape(1, edges)
    fwd, bwd = expand(wigner[0, 0])
    sources = source_forward(src, source_feats, fwd, weights)
    *lefts, tile_tgt = target_work(tgt, count, fwd, bwd, weights, sources, pieces)
    tile_src = source_back(src, count, bwd, weights, lefts, rows)

    parts = tile_tgt.reshape(inner, outer, COEF, 8, C)
    summed = parts[0].astype(F32)
    for d in range(1, inner):
        got = exchange(parts[d], "col", d)
        summed = summed + got.astype(F32)
    sent = summed.astype(BF16)
    result = summed[0]
    for d in range(1, outer):
        got = exchange(sent[d], "col", inner * d)
        result = result + got.astype(F32)
    result = result + tile_src[0].astype(F32)
    for d in range(1, rows):
        result = result + exchange(tile_src[d], "row", d).astype(F32)
    return result.transpose(1, 0, 2)


def solution(mesh):
    placed = (
        P(("row", "col"), None, None),
        P(("row", "col"), None, None),
        P("row", "col", None),
        P("row", "col", None),
        P("row", "col"),
        P("row", "col", None, None),
        P(),
        P(),
        P(),
    )
    return jax.shard_map(
        step, mesh=mesh, in_specs=placed, out_specs=P(("row", "col"), None, None), check_vma=False
    )
```

```python
import functools

import jax
import jax.numpy as jnp
from jax import lax
from jax.experimental import pallas as pl
from jax.experimental.pallas import tpu as pltpu
from jax.sharding import PartitionSpec as P


C = 128
COEF = 25
ROWS = 19
GROUP = 8
K_PAD = 20 * GROUP
J_PAD = 26 * GROUP
SLOTS = (0, 1, 2, 3, 4, -1, 5, 6, 7, 8, 9, 10, 11, 12, 13, 14, 15, -1, 16, 17, 18, -1)
LANES = 256
INNER = 4
CHUNK = 256
F32 = jnp.float32
BF16 = jnp.bfloat16
MIB = 1024 * 1024
NT = (((1,), (1,)), ((), ()))


def iota(shape, axis):
    return lax.broadcasted_iota(jnp.int32, shape, axis)


def flatten(wig_ref, flat):
    flat[:, 384:512] = jnp.zeros((wig_ref.shape[0], 128), BF16)
    flat[:, 0 : wig_ref.shape[1]] = wig_ref[...]


def picked(operand, wanted):
    edges, depth = operand.shape
    same_edge = (iota((edges, LANES), 0) % GROUP) == (iota((edges, LANES), 1) % GROUP)
    chosen = jnp.where(iota((depth, LANES), 0) == wanted, 1.0, 0.0).astype(BF16)
    spread = jnp.dot(operand, chosen, preferred_element_type=F32)
    return jnp.where(same_edge, spread, 0.0).reshape(edges // GROUP, GROUP, LANES)


def expand_fwd_kernel(wig_ref, fwd_ref, flat):
    flatten(wig_ref, flat)
    slot = iota((256, LANES), 1) // GROUP

    def fwd_step(pair, unused):
        parts = []
        for odd in range(2):
            k = pair * 2 + odd
            base = jnp.minimum(k * COEF // 128, 2) * 128
            wanted = jnp.where((slot < COEF) & (k < ROWS), k * COEF + slot - base, -1)
            parts.append(picked(flat[:, pl.ds(aligned(base, 128), 256)], wanted))
        start = aligned(pair * 16, 16)
        fwd_ref[:, pl.ds(start, 16), :] = jnp.concatenate(parts, axis=1).astype(BF16)
        return unused

    lax.fori_loop(0, K_PAD // 16, fwd_step, 0)


def expand_bwd_kernel(wig_ref, bwd_ref, flat):
    flatten(wig_ref, flat)
    slot = iota((1, LANES), 1) // GROUP
    row_of = jnp.full(slot.shape, -1, jnp.int32)
    for n, k in enumerate(SLOTS):
        row_of = jnp.where(slot == n, k, row_of)

    def bwd_step(pair, unused):
        parts = []
        for odd in range(2):
            j = pair * 2 + odd
            wanted = jnp.where((row_of >= 0) & (j < COEF), row_of * COEF + j, -1)
            parts.append(picked(flat[...], wanted))
        start = aligned(pair * 16, 16)
        bwd_ref[:, pl.ds(start, 16), :] = jnp.concatenate(parts, axis=1).astype(BF16)
        return unused

    lax.fori_loop(0, J_PAD // 16, bwd_step, 0)


def aligned(value, by):
    return pl.multiple_of(value, by)


def fill_table(blocks, table, kinds):
    width = kinds * C
    for j in range(COEF):
        for kind in range(kinds):
            column = jnp.concatenate([block(kind, j).astype(F32) for block in blocks], axis=0)
            start = j * width + kind * C
            table[:, start : start + C] = column.astype(BF16)


def source_hot(ids_ref, chunk, atoms):
    ids = ids_ref[:, pl.ds(aligned(chunk * CHUNK, CHUNK), CHUNK)]
    place = ids ^ (lax.axis_index("row") * 8)
    return place == iota((atoms, CHUNK), 0)


def target_hot(ids_ref, chunk, atoms):
    ids = ids_ref[:, pl.ds(aligned(chunk * CHUNK, CHUNK), CHUNK)]
    place = ids ^ (lax.axis_index("col") * 8)
    block = place // 8
    outer = atoms // (8 * INNER)
    place = ((block % INNER) * outer + block // INNER) * 8 + place % 8
    return place == iota((atoms, CHUNK), 0)


def store_pair(packed, slot, first, second):
    groups = packed.shape[0]
    first = first.reshape(groups, GROUP, -1)
    second = second.reshape(groups, GROUP, -1)
    rows = slice(slot * GROUP, slot * GROUP + 2 * GROUP)
    packed[:, rows, :] = jnp.concatenate([first, second], axis=1).astype(BF16)


def clear_rows(packed, slots):
    groups, rows, width = packed.shape
    for g in range(groups):
        packed[g, slots * GROUP :, :] = jnp.zeros((rows - slots * GROUP, width), packed.dtype)


def gather_atoms(hot, table, packed):
    hot = jnp.where(hot, 1.0, 0.0).T.astype(BF16)
    width = packed.shape[2]
    for j in range(0, COEF, 2):
        count = min(2, COEF - j)
        value = jnp.dot(
            hot, table[:, j * width : (j + count) * width], preferred_element_type=F32
        )
        first = value[:, :width]
        second = value[:, width:] if count == 2 else jnp.zeros_like(first)
        store_pair(packed, j, first, second)


def rotate_group(rot_ref, g, packed, local_g):
    return jnp.dot(rot_ref[g], packed[local_g], preferred_element_type=F32)


def pair_row(first, second, k, kind=0):
    lanes = slice(kind * C, (kind + 1) * C)
    return jnp.concatenate([first[k * 8 : k * 8 + 8, lanes], second[k * 8 : k * 8 + 8, lanes]], 0)


def store_forward(value, lefts, top, low):
    for k in range(5):
        lefts[0][top, k * C : (k + 1) * C] = value(k).astype(BF16)
    for left, base, count in ((lefts[1], 5, 4), (lefts[2], 13, 3)):
        for n in range(count):
            p, q = value(base + n), value(base + count + n)
            here = slice(n * C, (n + 1) * C)
            there = slice((count + n) * C, (count + n + 1) * C)
            left[top, here] = p.astype(BF16)
            left[top, there] = (-q).astype(BF16)
            left[low, here] = q.astype(BF16)
            left[low, there] = p.astype(BF16)


def half_weight(w_ref, n, half):
    width = w_ref.shape[-1]
    if n == 0:
        return w_ref[:, half].reshape(-1, width)
    return w_ref[:, :, half].reshape(-1, width)


def source_forward_kernel(*refs):
    ids_ref, feats_ref, rot_ref = refs[:3]
    w_refs, outs = refs[3:6], refs[6:9]
    table, packed, lefts = refs[9], refs[10], refs[11:]
    edges = ids_ref.shape[1]
    blocks = [lambda kind, j, b=b: feats_ref[b, j] for b in range(feats_ref.shape[0])]
    fill_table(blocks, table, 1)
    clear_rows(packed, COEF + 1)

    def chunk_step(chunk, unused):
        gather_atoms(source_hot(ids_ref, chunk, table.shape[0]), table, packed)

        for g in range(0, CHUNK // GROUP, 2):
            at = chunk * (CHUNK // GROUP) + g
            pair = [rotate_group(rot_ref, at + n, packed, g + n) for n in range(2)]
            top, low = slice(g * 8, g * 8 + 16), slice(CHUNK + g * 8, CHUNK + g * 8 + 16)
            store_forward(lambda k: pair_row(*pair, k), lefts, top, low)
        for n in range(3):
            rows = lefts[n].shape[0]
            outs[n][pl.ds(aligned(chunk * rows, rows), rows), :] = jnp.dot(
                lefts[n][...], half_weight(w_refs[n], n, 0), preferred_element_type=F32
            )
        return unused

    lax.fori_loop(0, edges // CHUNK, chunk_step, 0)


def y_slices(start):
    out = [(0, start, k) for k in range(5)]
    for which, count in ((1, 4), (2, 3)):
        for sign in range(2):
            out += [(which, start + sign * CHUNK, n) for n in range(count)]
    return out


def back_half(half, chunk, lefts, w_refs, rot_ref, packed, edge_grad):
    for n, count, slot in ((0, 5, 0), (1, 4, 6), (2, 3, 14)):
        width = w_refs[n].shape[-1]
        rows = CHUNK if n == 0 else 2 * CHUNK
        here = pl.ds(aligned(chunk * rows, rows), rows)
        for k in range(0, count, 2):
            until = min(k + 2, count)
            if n == 0:
                weight = w_refs[n][k:until, half].reshape(-1, width)
                value = lax.dot_general(lefts[n][here, :], weight, NT, preferred_element_type=F32)
            else:
                real = w_refs[n][0, k:until, half].reshape(-1, width)
                imag = w_refs[n][1, k:until, half].reshape(-1, width)
                value = lax.dot_general(
                    lefts[n][here, :width], real, NT, preferred_element_type=F32
                ) + lax.dot_general(lefts[n][here, width:], imag, NT, preferred_element_type=F32)
            for sign in range(rows // CHUNK):
                part = value[sign * CHUNK : (sign + 1) * CHUNK]
                first = part[:, :C]
                second = part[:, C:] if until - k == 2 else jnp.zeros_like(first)
                store_pair(packed, slot + sign * (count + 1) // 2 * 2 + k, first, second)

    at = chunk * (CHUNK // GROUP)
    for g in range(0, CHUNK // GROUP, 2):
        pair = [rotate_group(rot_ref, at + g + n, packed, g + n) for n in range(2)]
        for j in range(COEF):
            edge_grad[g * 8 : g * 8 + 16, j * C : (j + 1) * C] = pair_row(*pair, j).astype(BF16)


def scatter_atoms(hot, count_ref, chunk, edge_grad, total):
    valid = chunk * CHUNK + iota(hot.shape, 1) < count_ref[0, 0]
    hot = jnp.where(hot & valid, 1.0, 0.0).astype(BF16)
    step = total.shape[1] // 5
    for n in range(5):
        here = slice(n * step, (n + 1) * step)
        total[:, here] += jnp.dot(hot, edge_grad[:, here], preferred_element_type=F32)


def write_blocks(total, out_ref):
    for j in range(COEF):
        for b in range(out_ref.shape[0]):
            out_ref[b, j] = total[b * 8 : b * 8 + 8, j * C : (j + 1) * C].astype(out_ref.dtype)


def target_kernel(count_pieces, *refs):
    ids_ref, count_ref, fwd_ref, bwd_ref = refs[:4]
    w_refs, sources = refs[4:7], refs[7:10]
    pieces = refs[10 : 10 + count_pieces]
    refs = refs[10 + count_pieces :]
    lefts, out_ref = refs[:3], refs[3]
    table, packed = refs[4], refs[5]
    forward_lefts, cots, ys, packed_back = refs[6:9], refs[9], refs[10:13], refs[13]
    edge_grad, total = refs[14], refs[15]
    edges = ids_ref.shape[1]
    blocks = []
    for piece in pieces:
        for b in range(piece.shape[0]):
            blocks.append(lambda kind, j, piece=piece, b=b: piece[b, kind, j])
    fill_table(blocks, table, 2)
    clear_rows(packed, COEF + 1)
    clear_rows(packed_back, len(SLOTS))
    total[...] = jnp.zeros_like(total)

    def chunk_step(chunk, unused):
        hot = target_hot(ids_ref, chunk, table.shape[0])
        gather_atoms(hot, table, packed)

        for g in range(0, CHUNK // GROUP, 2):
            at = chunk * (CHUNK // GROUP) + g
            pair = [rotate_group(fwd_ref, at + n, packed, g + n) for n in range(2)]
            top, low = slice(g * 8, g * 8 + 16), slice(CHUNK + g * 8, CHUNK + g * 8 + 16)
            store_forward(lambda k: pair_row(*pair, k), forward_lefts, top, low)
            for k in range(ROWS):
                cots[top, k * C : (k + 1) * C] = pair_row(*pair, k, 1).astype(BF16)
        for n in range(3):
            rows = forward_lefts[n].shape[0]
            ys[n][...] = sources[n][pl.ds(aligned(chunk * rows, rows), rows), :] + jnp.dot(
                forward_lefts[n][...], half_weight(w_refs[n], n, 1), preferred_element_type=F32
            )

        def gate(i, unused):
            start = aligned(i * 16, 16)
            top = pl.ds(start, 16)
            cot = [cots[top, k * C : (k + 1) * C].astype(F32) for k in range(ROWS)]
            where = y_slices(start)

            def y_at(k):
                which, row, n = where[k]
                return ys[which][pl.ds(aligned(row, 16), 16), n * C : (n + 1) * C]

            y0 = y_at(0)
            gating = jax.nn.sigmoid(y0)
            slope = gating * (1.0 - gating)
            dotted = cot[1] * y_at(1)
            for k in range(2, ROWS):
                dotted = dotted + cot[k] * y_at(k)
            grads = [cot[0] * (gating + y0 * slope) + dotted * slope]
            grads += [gating * cot[k] for k in range(1, ROWS)]
            zero_row = aligned(chunk * CHUNK + start, 16)
            top_row = aligned(chunk * 2 * CHUNK + start, 16)
            low_row = aligned(chunk * 2 * CHUNK + CHUNK + start, 16)
            store_backward(grads, lefts, zero_row, top_row, low_row)
            return unused

        lax.fori_loop(0, CHUNK // 16, gate, 0, unroll=4)
        back_half(1, chunk, lefts, w_refs, bwd_ref, packed_back, edge_grad)
        hot = target_hot(ids_ref, chunk, table.shape[0])
        scatter_atoms(hot, count_ref, chunk, edge_grad, total)
        return unused

    lax.fori_loop(0, edges // CHUNK, chunk_step, 0)
    write_blocks(total, out_ref)


def store_backward(value, lefts, zero_row, top_row, low_row):
    for k in range(5):
        lefts[0][pl.ds(zero_row, 16), k * C : (k + 1) * C] = value[k].astype(BF16)
    top, low = pl.ds(top_row, 16), pl.ds(low_row, 16)
    for left, base, count in ((lefts[1], 5, 4), (lefts[2], 13, 3)):
        for n in range(count):
            a, b = value[base + n], value[base + count + n]
            here = slice(n * C, (n + 1) * C)
            there = slice((count + n) * C, (count + n + 1) * C)
            left[top, here] = a.astype(BF16)
            left[top, there] = b.astype(BF16)
            left[low, here] = b.astype(BF16)
            left[low, there] = (-a).astype(BF16)


def source_back_kernel(*refs):
    ids_ref, count_ref, bwd_ref = refs[:3]
    w_refs, lefts, out_ref = refs[3:6], refs[6:9], refs[9]
    packed, edge_grad, total = refs[10:]
    clear_rows(packed, len(SLOTS))
    total[...] = jnp.zeros_like(total)

    def chunk_step(chunk, unused):
        back_half(0, chunk, lefts, w_refs, bwd_ref, packed, edge_grad)
        scatter_atoms(source_hot(ids_ref, chunk, total.shape[0]), count_ref, chunk, edge_grad, total)
        return unused

    lax.fori_loop(0, lefts[0].shape[0] // CHUNK, chunk_step, 0)
    write_blocks(total, out_ref)


IN_VMEM = pl.BlockSpec(memory_space=pltpu.VMEM)
IN_SMEM = pl.BlockSpec(memory_space=pltpu.SMEM)


def call(kernel, args, outs, scratch, limit, flops, scalar=None):
    moved = sum(a.size * a.dtype.itemsize for a in (*args, *outs))
    return pl.pallas_call(
        kernel,
        in_specs=[IN_SMEM if n == scalar else IN_VMEM for n in range(len(args))],
        out_specs=[IN_VMEM] * len(outs),
        out_shape=outs,
        scratch_shapes=[pltpu.VMEM(s, d) for s, d in scratch],
        compiler_params=pltpu.CompilerParams(vmem_limit_bytes=limit * MIB),
        cost_estimate=pl.CostEstimate(flops=flops, bytes_accessed=moved, transcendentals=0),
    )(*args)


def arrays(shapes, dtype):
    return [jax.ShapeDtypeStruct(s, dtype) for s in shapes]


def y_shapes(edges):
    return [(edges, 5 * C), (2 * edges, 4 * C), (2 * edges, 3 * C)]


def left_shapes(edges):
    return [(edges, 5 * C), (2 * edges, 8 * C), (2 * edges, 6 * C)]


def typed(shapes, dtype):
    return [(s, dtype) for s in shapes]


def packed_shape(kinds):
    return (CHUNK // GROUP, LANES, kinds * C)


PUSH = 2 * 65536


def expand(kernel, rows, wig):
    edges = wig.shape[0]
    outs = arrays([(edges // GROUP, rows, LANES)], BF16)
    return call(kernel, [wig], outs, [((edges, 512), BF16)], 6, PUSH * edges * 40)[0]


def source_forward(ids, feats, rot, weights):
    edges = ids.shape[1]
    scratch = [((feats.shape[0] * 8, COEF * C), BF16), (packed_shape(1), BF16)]
    scratch += typed(left_shapes(CHUNK), BF16)
    return call(
        source_forward_kernel,
        [ids, feats, rot, *weights],
        arrays(y_shapes(edges), F32),
        scratch,
        12,
        PUSH * edges * 64,
    )


def target_work(ids, count, fwd, bwd, weights, sources, pieces):
    edges = ids.shape[1]
    blocks = sum(p.shape[0] for p in pieces)
    outs = arrays(left_shapes(edges), BF16) + arrays([(blocks, COEF, 8, C)], BF16)
    scratch = [((blocks * 8, 2 * COEF * C), BF16), (packed_shape(2), BF16)]
    scratch += typed(left_shapes(CHUNK), BF16) + [((CHUNK, ROWS * C), BF16)]
    scratch += typed(y_shapes(CHUNK), F32) + [(packed_shape(1), BF16)]
    scratch += [((CHUNK, COEF * C), BF16), ((blocks * 8, COEF * C), F32)]
    return call(
        functools.partial(target_kernel, len(pieces)),
        [ids, count, fwd, bwd, *weights, *sources, *pieces],
        outs,
        scratch,
        21 + blocks // 4,
        PUSH * edges * 160,
        1,
    )


def source_back(ids, count, bwd, weights, lefts, blocks):
    scratch = [(packed_shape(1), BF16)]
    scratch += [((CHUNK, COEF * C), BF16), ((blocks * 8, COEF * C), F32)]
    return call(
        source_back_kernel,
        [ids, count, bwd, *weights, *lefts],
        arrays([(blocks, COEF, 8, C)], BF16),
        scratch,
        12,
        PUSH * lefts[0].shape[0] * 70,
        1,
    )[0]


def exchange(value, axis, distance):
    size = lax.axis_size(axis)
    return lax.ppermute(value, axis, [(i, i ^ distance) for i in range(size)])


def step(node_feats, grad_out, edge_src, edge_tgt, count, wigner, w_zero, w_one, w_two):
    rows, cols = lax.axis_size("row"), lax.axis_size("col")
    inner, outer = INNER, cols // INNER
    feats = node_feats.transpose(1, 0, 2)
    own = jnp.stack([feats, grad_out.transpose(1, 0, 2)])
    line = [own]
    for d in range(1, outer):
        line.append(exchange(own, "col", inner * d))
    line = jnp.stack(line)
    source_feats = [feats] + [exchange(feats, "row", d) for d in range(1, rows)]
    source_feats = jnp.stack(source_feats)
    first = exchange(line, "col", 1)
    second = exchange(line, "col", 2)
    far_first = exchange(first[: outer // 2], "col", 2)
    far_second = exchange(second[outer // 2 :], "col", 1)
    pieces = [line, first, second, far_first, far_second]

    weights = (
        w_zero.reshape(5, 2, C, 5 * C),
        w_one.reshape(2, 4, 2, C, 4 * C),
        w_two.reshape(2, 3, 2, C, 3 * C),
    )
    edges = edge_src.shape[-1]
    src, tgt = edge_src.reshape(1, edges), edge_tgt.reshape(1, edges)
    fwd = expand(expand_fwd_kernel, K_PAD, wigner[0, 0])
    bwd = expand(expand_bwd_kernel, J_PAD, wigner[0, 0])
    sources = source_forward(src, source_feats, fwd, weights)
    *lefts, tile_tgt = target_work(tgt, count, fwd, bwd, weights, sources, pieces)
    tile_src = source_back(src, count, bwd, weights, lefts, rows)

    parts = tile_tgt.reshape(inner, outer, COEF, 8, C)
    summed = parts[0].astype(F32)
    for d in range(1, inner):
        got = exchange(parts[d], "col", d)
        summed = summed + got.astype(F32)
    sent = summed.astype(BF16)
    result = summed[0]
    for d in range(1, outer):
        got = exchange(sent[d], "col", inner * d)
        result = result + got.astype(F32)
    result = result + tile_src[0].astype(F32)
    for d in range(1, rows):
        result = result + exchange(tile_src[d], "row", d).astype(F32)
    return result.transpose(1, 0, 2)


def solution(mesh):
    placed = (
        P(("row", "col"), None, None),
        P(("row", "col"), None, None),
        P("row", "col", None),
        P("row", "col", None),
        P("row", "col"),
        P("row", "col", None, None),
        P(),
        P(),
        P(),
    )
    return jax.shard_map(
        step, mesh=mesh, in_specs=placed, out_specs=P(("row", "col"), None, None), check_vma=False
    )
```

```python
import functools

import jax
import jax.numpy as jnp
from jax import lax
from jax.experimental import pallas as pl
from jax.experimental.pallas import tpu as pltpu
from jax.sharding import PartitionSpec as P


C = 128
COEF = 25
ROWS = 19
GROUP = 8
K_PAD = 20 * GROUP
J_PAD = 26 * GROUP
SLOTS = (0, 1, 2, 3, 4, -1, 5, 6, 7, 8, 9, 10, 11, 12, 13, 14, 15, -1, 16, 17, 18, -1)
LANES = 256
INNER = 4
CHUNK = 256
F32 = jnp.float32
BF16 = jnp.bfloat16
MIB = 1024 * 1024
NT = (((1,), (1,)), ((), ()))


def iota(shape, axis):
    return lax.broadcasted_iota(jnp.int32, shape, axis)


def flatten(wig_ref, tall, flat_ref):
    width = wig_ref.shape[0]
    tall[480:512, :] = jnp.zeros((32, tall.shape[1]), F32)
    tall[width // 8 * 8 : 480, :] = jnp.zeros((480 - width // 8 * 8, tall.shape[1]), F32)
    tall[0:width, :] = wig_ref[...].astype(F32)
    flat_ref[...] = tall[...].T.astype(BF16)


def picked(operand, wanted):
    edges, depth = operand.shape
    same_edge = (iota((edges, LANES), 0) % GROUP) == (iota((edges, LANES), 1) % GROUP)
    chosen = jnp.where(iota((depth, LANES), 0) == wanted, 1.0, 0.0).astype(BF16)
    spread = jnp.dot(operand, chosen, preferred_element_type=F32)
    return jnp.where(same_edge, spread, 0.0).reshape(edges // GROUP, GROUP, LANES)


def expand_fwd_kernel(wig_ref, fwd_ref, flat, tall):
    flatten(wig_ref, tall, flat)
    slot = iota((256, LANES), 1) // GROUP

    def fwd_step(pair, unused):
        parts = []
        for odd in range(2):
            k = pair * 2 + odd
            base = jnp.minimum(k * COEF // 128, 2) * 128
            wanted = jnp.where((slot < COEF) & (k < ROWS), k * COEF + slot - base, -1)
            parts.append(picked(flat[:, pl.ds(aligned(base, 128), 256)], wanted))
        start = aligned(pair * 16, 16)
        fwd_ref[:, pl.ds(start, 16), :] = jnp.concatenate(parts, axis=1).astype(BF16)
        return unused

    lax.fori_loop(0, K_PAD // 16, fwd_step, 0)


def expand_bwd_kernel(flat_ref, bwd_ref, flat):
    dest = iota((512, 512), 1)
    origin = jnp.where(dest < ROWS * COEF, dest % ROWS * COEF + dest // ROWS, -1)
    move = jnp.where(iota((512, 512), 0) == origin, 1.0, 0.0).astype(BF16)
    flat[...] = jnp.dot(flat_ref[...], move, preferred_element_type=F32).astype(BF16)
    slot = iota((1, LANES), 1) // GROUP
    row_of = jnp.full(slot.shape, -1, jnp.int32)
    for n, k in enumerate(SLOTS):
        row_of = jnp.where(slot == n, k, row_of)

    def bwd_step(pair, unused):
        parts = []
        for odd in range(2):
            j = pair * 2 + odd
            base = jnp.minimum(j * ROWS // 128, 2) * 128
            wanted = jnp.where((row_of >= 0) & (j < COEF), row_of + j * ROWS - base, -1)
            parts.append(picked(flat[:, pl.ds(aligned(base, 128), 256)], wanted))
        start = aligned(pair * 16, 16)
        bwd_ref[:, pl.ds(start, 16), :] = jnp.concatenate(parts, axis=1).astype(BF16)
        return unused

    lax.fori_loop(0, J_PAD // 16, bwd_step, 0)


def aligned(value, by):
    return pl.multiple_of(value, by)


def fill_table(blocks, table, kinds):
    width = kinds * C
    for j in range(COEF):
        for kind in range(kinds):
            column = jnp.concatenate([block(kind, j).astype(F32) for block in blocks], axis=0)
            start = j * width + kind * C
            table[:, start : start + C] = column.astype(BF16)


def source_hot(ids, atoms):
    place = ids ^ (lax.axis_index("row") * 8)
    return place == iota((atoms, ids.shape[1]), 0)


def target_hot(ids, atoms):
    place = ids ^ (lax.axis_index("col") * 8)
    block = place // 8
    outer = atoms // (8 * INNER)
    place = ((block % INNER) * outer + block // INNER) * 8 + place % 8
    return place == iota((atoms, ids.shape[1]), 0)


def store_pair(packed, slot, first, second):
    groups = packed.shape[0]
    first = first.reshape(groups, GROUP, -1)
    second = second.reshape(groups, GROUP, -1)
    rows = slice(slot * GROUP, slot * GROUP + 2 * GROUP)
    packed[:, rows, :] = jnp.concatenate([first, second], axis=1).astype(BF16)


def clear_rows(packed, slots):
    groups, rows, width = packed.shape
    for g in range(groups):
        packed[g, slots * GROUP :, :] = jnp.zeros((rows - slots * GROUP, width), packed.dtype)


def gather_atoms(hot, table, packed):
    hot = jnp.where(hot, 1.0, 0.0).T.astype(BF16)
    width = packed.shape[2]
    for j in range(0, COEF, 2):
        count = min(2, COEF - j)
        value = jnp.dot(
            hot, table[:, j * width : (j + count) * width], preferred_element_type=F32
        )
        first = value[:, :width]
        second = value[:, width:] if count == 2 else jnp.zeros_like(first)
        store_pair(packed, j, first, second)


def rotate_group(rot_ref, g, packed, local_g):
    return jnp.dot(rot_ref[g], packed[local_g], preferred_element_type=F32)


def pair_row(first, second, k, kind=0):
    lanes = slice(kind * C, (kind + 1) * C)
    return jnp.concatenate([first[k * 8 : k * 8 + 8, lanes], second[k * 8 : k * 8 + 8, lanes]], 0)


def store_forward(value, lefts, top, low):
    for k in range(5):
        lefts[0][top, k * C : (k + 1) * C] = value(k).astype(BF16)
    for left, base, count in ((lefts[1], 5, 4), (lefts[2], 13, 3)):
        for n in range(count):
            p, q = value(base + n), value(base + count + n)
            here = slice(n * C, (n + 1) * C)
            there = slice((count + n) * C, (count + n + 1) * C)
            left[top, here] = p.astype(BF16)
            left[top, there] = (-q).astype(BF16)
            left[low, here] = q.astype(BF16)
            left[low, there] = p.astype(BF16)


def half_weight(w_ref, n, half):
    width = w_ref.shape[-1]
    if n == 0:
        return w_ref[:, half].reshape(-1, width)
    return w_ref[:, :, half].reshape(-1, width)


def source_forward_kernel(count_pieces, *refs):
    ids_ref, rot_ref = refs[:2]
    w_refs, pieces = refs[2:5], refs[5 : 5 + count_pieces]
    refs = refs[5 + count_pieces :]
    outs, table, packed, lefts = refs[:3], refs[3], refs[4], refs[5:]
    edges = ids_ref.shape[1]
    blocks = [lambda kind, j, piece=piece: piece[j] for piece in pieces]
    fill_table(blocks, table, 1)
    clear_rows(packed, COEF + 1)

    gather_atoms(source_hot(ids_ref[...], table.shape[0]), table, packed)
    for g in range(0, edges // GROUP, 2):
        pair = [rotate_group(rot_ref, g + n, packed, g + n) for n in range(2)]
        top, low = slice(g * 8, g * 8 + 16), slice(edges + g * 8, edges + g * 8 + 16)
        store_forward(lambda k: pair_row(*pair, k), lefts, top, low)
    for n in range(3):
        outs[n][...] = jnp.dot(
            lefts[n][...], half_weight(w_refs[n], n, 0), preferred_element_type=F32
        )


def y_slices(start):
    out = [(0, start, k) for k in range(5)]
    for which, count in ((1, 4), (2, 3)):
        for sign in range(2):
            out += [(which, start + sign * CHUNK, n) for n in range(count)]
    return out


def back_half(half, first, lefts, w_refs, rot_ref, packed, edge_grad):
    groups = packed.shape[0]
    count = groups * GROUP
    edges = lefts[0].shape[0]
    for n, terms, slot in ((0, 5, 0), (1, 4, 6), (2, 3, 14)):
        width = w_refs[n].shape[-1]
        for k in range(0, terms, 2):
            until = min(k + 2, terms)
            for sign in range(1 if n == 0 else 2):
                here = pl.ds(aligned(first + sign * edges, GROUP), count)
                if n == 0:
                    weight = w_refs[n][k:until, half].reshape(-1, width)
                    value = lax.dot_general(
                        lefts[n][here, :], weight, NT, preferred_element_type=F32
                    )
                else:
                    real = w_refs[n][0, k:until, half].reshape(-1, width)
                    imag = w_refs[n][1, k:until, half].reshape(-1, width)
                    value = lax.dot_general(
                        lefts[n][here, :width], real, NT, preferred_element_type=F32
                    ) + lax.dot_general(
                        lefts[n][here, width:], imag, NT, preferred_element_type=F32
                    )
                one = value[:, :C]
                two = value[:, C:] if until - k == 2 else jnp.zeros_like(one)
                store_pair(packed, slot + sign * (terms + 1) // 2 * 2 + k, one, two)

    at = first // GROUP
    for g in range(0, groups, 2):
        pair = [rotate_group(rot_ref, at + g + n, packed, g + n) for n in range(2)]
        rows = pl.ds(aligned(first + g * 8, 16), 16)
        for j in range(COEF):
            edge_grad[rows, j * C : (j + 1) * C] = pair_row(*pair, j).astype(BF16)


def scatter_atoms(hot, count_ref, edge_grad, out_ref):
    valid = iota(hot.shape, 1) < count_ref[0, 0]
    hot = jnp.where(hot & valid, 1.0, 0.0).astype(BF16)
    for j in range(0, COEF, 2):
        until = min(j + 2, COEF)
        total = jnp.dot(hot, edge_grad[:, j * C : until * C], preferred_element_type=F32)
        for n in range(until - j):
            for b in range(out_ref.shape[0]):
                block = total[b * 8 : b * 8 + 8, n * C : (n + 1) * C]
                out_ref[b, j + n] = block.astype(out_ref.dtype)


def target_kernel(count_pieces, *refs):
    ids_ref, count_ref, fwd_ref, bwd_ref = refs[:4]
    w_refs, sources = refs[4:7], refs[7:10]
    pieces = refs[10 : 10 + count_pieces]
    refs = refs[10 + count_pieces :]
    lefts, out_ref = refs[:3], refs[3]
    table, packed = refs[4], refs[5]
    forward_lefts, cots, ys, packed_back = refs[6:9], refs[9], refs[10:13], refs[13]
    edge_grad = refs[14]
    edges = ids_ref.shape[1]
    blocks = []
    for piece in pieces:
        for b in range(piece.shape[0]):
            blocks.append(lambda kind, j, piece=piece, b=b: piece[b, kind, j])
    fill_table(blocks, table, 2)
    clear_rows(packed, COEF + 1)
    clear_rows(packed_back, len(SLOTS))

    def chunk_step(chunk, unused):
        first = aligned(chunk * CHUNK, CHUNK)
        hot = target_hot(ids_ref[:, pl.ds(first, CHUNK)], table.shape[0])
        gather_atoms(hot, table, packed)

        for g in range(0, CHUNK // GROUP, 2):
            at = chunk * (CHUNK // GROUP) + g
            pair = [rotate_group(fwd_ref, at + n, packed, g + n) for n in range(2)]
            top, low = slice(g * 8, g * 8 + 16), slice(CHUNK + g * 8, CHUNK + g * 8 + 16)
            store_forward(lambda k: pair_row(*pair, k), forward_lefts, top, low)
            for k in range(ROWS):
                cots[top, k * C : (k + 1) * C] = pair_row(*pair, k, 1).astype(BF16)
        for n in range(3):
            value = jnp.dot(
                forward_lefts[n][...], half_weight(w_refs[n], n, 1), preferred_element_type=F32
            )
            for sign in range(1 if n == 0 else 2):
                here = slice(sign * CHUNK, (sign + 1) * CHUNK)
                there = pl.ds(aligned(first + sign * edges, CHUNK), CHUNK)
                ys[n][here, :] = sources[n][there, :] + value[here]

        def gate(i, unused):
            start = aligned(i * 16, 16)
            top = pl.ds(start, 16)
            cot = [cots[top, k * C : (k + 1) * C].astype(F32) for k in range(ROWS)]
            where = y_slices(start)

            def y_at(k):
                which, row, n = where[k]
                return ys[which][pl.ds(aligned(row, 16), 16), n * C : (n + 1) * C]

            y0 = y_at(0)
            gating = jax.nn.sigmoid(y0)
            slope = gating * (1.0 - gating)
            dotted = cot[1] * y_at(1)
            for k in range(2, ROWS):
                dotted = dotted + cot[k] * y_at(k)
            grads = [cot[0] * (gating + y0 * slope) + dotted * slope]
            grads += [gating * cot[k] for k in range(1, ROWS)]
            store_backward(grads, lefts, first + start)
            return unused

        lax.fori_loop(0, CHUNK // 16, gate, 0, unroll=True)
        back_half(1, first, lefts, w_refs, bwd_ref, packed_back, edge_grad)
        return unused

    lax.fori_loop(0, edges // CHUNK, chunk_step, 0)
    scatter_atoms(target_hot(ids_ref[...], table.shape[0]), count_ref, edge_grad, out_ref)


def store_backward(value, lefts, row):
    top = pl.ds(aligned(row, 16), 16)
    low = pl.ds(aligned(row + lefts[0].shape[0], 16), 16)
    for k in range(5):
        lefts[0][top, k * C : (k + 1) * C] = value[k].astype(BF16)
    for left, base, count in ((lefts[1], 5, 4), (lefts[2], 13, 3)):
        for n in range(count):
            a, b = value[base + n], value[base + count + n]
            here = slice(n * C, (n + 1) * C)
            there = slice((count + n) * C, (count + n + 1) * C)
            left[top, here] = a.astype(BF16)
            left[top, there] = b.astype(BF16)
            left[low, here] = b.astype(BF16)
            left[low, there] = (-a).astype(BF16)


def source_back_kernel(*refs):
    ids_ref, count_ref, bwd_ref = refs[:3]
    w_refs, lefts, out_ref = refs[3:6], refs[6:9], refs[9]
    packed, edge_grad = refs[10:]
    clear_rows(packed, len(SLOTS))
    back_half(0, 0, lefts, w_refs, bwd_ref, packed, edge_grad)
    scatter_atoms(source_hot(ids_ref[...], out_ref.shape[0] * 8), count_ref, edge_grad, out_ref)


IN_VMEM = pl.BlockSpec(memory_space=pltpu.VMEM)
IN_SMEM = pl.BlockSpec(memory_space=pltpu.SMEM)


def call(kernel, args, outs, scratch, limit, flops, scalar=None):
    moved = sum(a.size * a.dtype.itemsize for a in (*args, *outs))
    return pl.pallas_call(
        kernel,
        in_specs=[IN_SMEM if n == scalar else IN_VMEM for n in range(len(args))],
        out_specs=[IN_VMEM] * len(outs),
        out_shape=outs,
        scratch_shapes=[pltpu.VMEM(s, d) for s, d in scratch],
        compiler_params=pltpu.CompilerParams(vmem_limit_bytes=limit * MIB),
        cost_estimate=pl.CostEstimate(flops=flops, bytes_accessed=moved, transcendentals=0),
    )(*args)


def arrays(shapes, dtype):
    return [jax.ShapeDtypeStruct(s, dtype) for s in shapes]


def y_shapes(edges):
    return [(edges, 5 * C), (2 * edges, 4 * C), (2 * edges, 3 * C)]


def left_shapes(edges):
    return [(edges, 5 * C), (2 * edges, 8 * C), (2 * edges, 6 * C)]


def typed(shapes, dtype):
    return [(s, dtype) for s in shapes]


def packed_shape(edges, kinds):
    return (edges // GROUP, LANES, kinds * C)


PUSH = 2 * 65536


def expand_fwd(tall):
    edges = tall.shape[1]
    outs = arrays([(edges // GROUP, K_PAD, LANES), (edges, 512)], BF16)
    scratch = [((512, edges), F32)]
    return call(expand_fwd_kernel, [tall], outs, scratch, 6, PUSH * edges * 20)


def expand_bwd(flat):
    edges = flat.shape[0]
    outs = arrays([(edges // GROUP, J_PAD, LANES)], BF16)
    return call(expand_bwd_kernel, [flat], outs, [((edges, 512), BF16)], 6, PUSH * edges * 30)[0]


def source_forward(ids, pieces, rot, weights):
    edges = ids.shape[1]
    scratch = [((len(pieces) * 8, COEF * C), BF16), (packed_shape(edges, 1), BF16)]
    scratch += typed(left_shapes(edges), BF16)
    return call(
        functools.partial(source_forward_kernel, len(pieces)),
        [ids, rot, *weights, *pieces],
        arrays(y_shapes(edges), F32),
        scratch,
        14,
        PUSH * edges * 64,
    )


def target_work(ids, count, fwd, bwd, weights, sources, pieces):
    edges = ids.shape[1]
    blocks = sum(p.shape[0] for p in pieces)
    outs = arrays(left_shapes(edges), BF16) + arrays([(blocks, COEF, 8, C)], BF16)
    scratch = [((blocks * 8, 2 * COEF * C), BF16), (packed_shape(CHUNK, 2), BF16)]
    scratch += typed(left_shapes(CHUNK), BF16) + [((CHUNK, ROWS * C), BF16)]
    scratch += typed(y_shapes(CHUNK), F32) + [(packed_shape(CHUNK, 1), BF16)]
    scratch += [((edges, COEF * C), BF16)]
    return call(
        functools.partial(target_kernel, len(pieces)),
        [ids, count, fwd, bwd, *weights, *sources, *pieces],
        outs,
        scratch,
        21 + blocks // 4,
        PUSH * edges * 160,
        1,
    )


def source_back(ids, count, bwd, weights, lefts, blocks):
    edges = lefts[0].shape[0]
    scratch = [(packed_shape(edges, 1), BF16), ((edges, COEF * C), BF16)]
    return call(
        source_back_kernel,
        [ids, count, bwd, *weights, *lefts],
        arrays([(blocks, COEF, 8, C)], BF16),
        scratch,
        12,
        PUSH * edges * 70,
        1,
    )[0]


def exchange(value, axis, distance):
    size = lax.axis_size(axis)
    return lax.ppermute(value, axis, [(i, i ^ distance) for i in range(size)])


def step(node_feats, grad_out, edge_src, edge_tgt, count, wigner, w_zero, w_one, w_two):
    rows, cols = lax.axis_size("row"), lax.axis_size("col")
    inner, outer = INNER, cols // INNER
    feats = node_feats.transpose(1, 0, 2)
    own = jnp.stack([feats, grad_out.transpose(1, 0, 2)])
    line = []
    for d in range(1, outer):
        line.append(exchange(own, "col", inner * d))
    own_first = exchange(own, "col", 1)
    own_second = exchange(own, "col", 2)
    source_feats = [feats] + [exchange(feats, "row", d) for d in range(1, rows)]
    line = jnp.stack(line)
    first = exchange(line, "col", 1)
    second = exchange(line, "col", 2)
    cut = outer // 2
    far_first = exchange(first[:cut], "col", 2)
    rest = jnp.concatenate([own_second[None], second[cut:]])
    far_second = exchange(rest, "col", 1)
    pieces = [own[None], line, own_first[None], first, own_second[None], second]
    pieces += [far_second[:1], far_first, far_second[1:]]

    weights = (
        w_zero.reshape(5, 2, C, 5 * C),
        w_one.reshape(2, 4, 2, C, 4 * C),
        w_two.reshape(2, 3, 2, C, 3 * C),
    )
    edges = edge_src.shape[-1]
    src, tgt = edge_src.reshape(1, edges), edge_tgt.reshape(1, edges)
    fwd, flat = expand_fwd(wigner[0, 0].T)
    bwd = expand_bwd(flat)
    sources = source_forward(src, source_feats, fwd, weights)
    *lefts, tile_tgt = target_work(tgt, count, fwd, bwd, weights, sources, pieces)
    tile_src = source_back(src, count, bwd, weights, lefts, rows)

    parts = tile_tgt.reshape(inner, outer, COEF, 8, C)
    summed = parts[0].astype(F32)
    for d in range(1, inner):
        got = exchange(parts[d], "col", d)
        summed = summed + got.astype(F32)
    sent = summed.astype(BF16)
    result = summed[0]
    for d in range(1, outer):
        got = exchange(sent[d], "col", inner * d)
        result = result + got.astype(F32)
    result = result + tile_src[0].astype(F32)
    for d in range(1, rows):
        result = result + exchange(tile_src[d], "row", d).astype(F32)
    return result.transpose(1, 0, 2)


def solution(mesh):
    placed = (
        P(("row", "col"), None, None),
        P(("row", "col"), None, None),
        P("row", "col", None),
        P("row", "col", None),
        P("row", "col"),
        P("row", "col", None, None),
        P(),
        P(),
        P(),
    )
    return jax.shard_map(
        step, mesh=mesh, in_specs=placed, out_specs=P(("row", "col"), None, None), check_vma=False
    )
```

```python
import functools

import jax
import jax.numpy as jnp
from jax import lax
from jax.experimental import pallas as pl
from jax.experimental.pallas import tpu as pltpu
from jax.sharding import PartitionSpec as P


C = 128
COEF = 25
ROWS = 19
GROUP = 8
K_PAD = 20 * GROUP
J_PAD = 26 * GROUP
SLOTS = (0, 1, 2, 3, 4, -1, 5, 6, 7, 8, 9, 10, 11, 12, 13, 14, 15, -1, 16, 17, 18, -1)
LANES = 256
INNER = 4
CHUNK = 256
F32 = jnp.float32
BF16 = jnp.bfloat16
MIB = 1024 * 1024
NT = (((1,), (1,)), ((), ()))


def iota(shape, axis):
    return lax.broadcasted_iota(jnp.int32, shape, axis)


def flatten(wig_ref, tall, flat_ref):
    width = wig_ref.shape[0]
    tall[480:512, :] = jnp.zeros((32, tall.shape[1]), F32)
    tall[width // 8 * 8 : 480, :] = jnp.zeros((480 - width // 8 * 8, tall.shape[1]), F32)
    tall[0:width, :] = wig_ref[...].astype(F32)
    flat_ref[...] = tall[...].T.astype(BF16)


def picked(operand, wanted):
    edges, depth = operand.shape
    same_edge = (iota((edges, LANES), 0) % GROUP) == (iota((edges, LANES), 1) % GROUP)
    chosen = jnp.where(iota((depth, LANES), 0) == wanted, 1.0, 0.0).astype(BF16)
    spread = jnp.dot(operand, chosen, preferred_element_type=F32)
    return jnp.where(same_edge, spread, 0.0).reshape(edges // GROUP, GROUP, LANES)


def expand_fwd_kernel(wig_ref, fwd_ref, flat, tall):
    flatten(wig_ref, tall, flat)
    slot = iota((256, LANES), 1) // GROUP

    def fwd_step(pair, unused):
        parts = []
        for odd in range(2):
            k = pair * 2 + odd
            base = jnp.minimum(k * COEF // 128, 2) * 128
            wanted = jnp.where((slot < COEF) & (k < ROWS), k * COEF + slot - base, -1)
            parts.append(picked(flat[:, pl.ds(aligned(base, 128), 256)], wanted))
        start = aligned(pair * 16, 16)
        fwd_ref[:, pl.ds(start, 16), :] = jnp.concatenate(parts, axis=1).astype(BF16)
        return unused

    lax.fori_loop(0, K_PAD // 16, fwd_step, 0, unroll=True)


def expand_bwd_kernel(flat_ref, bwd_ref, flat):
    dest = iota((512, 512), 1)
    origin = jnp.where(dest < ROWS * COEF, dest % ROWS * COEF + dest // ROWS, -1)
    move = jnp.where(iota((512, 512), 0) == origin, 1.0, 0.0).astype(BF16)
    flat[...] = jnp.dot(flat_ref[...], move, preferred_element_type=F32).astype(BF16)
    slot = iota((1, LANES), 1) // GROUP
    row_of = jnp.full(slot.shape, -1, jnp.int32)
    for n, k in enumerate(SLOTS):
        row_of = jnp.where(slot == n, k, row_of)

    def bwd_step(pair, unused):
        parts = []
        for odd in range(2):
            j = pair * 2 + odd
            base = jnp.minimum(j * ROWS // 128, 2) * 128
            wanted = jnp.where((row_of >= 0) & (j < COEF), row_of + j * ROWS - base, -1)
            parts.append(picked(flat[:, pl.ds(aligned(base, 128), 256)], wanted))
        start = aligned(pair * 16, 16)
        bwd_ref[:, pl.ds(start, 16), :] = jnp.concatenate(parts, axis=1).astype(BF16)
        return unused

    lax.fori_loop(0, J_PAD // 16, bwd_step, 0, unroll=True)


def aligned(value, by):
    return pl.multiple_of(value, by)


def fill_table(blocks, table, kinds):
    width = kinds * C
    for j in range(COEF):
        for kind in range(kinds):
            column = jnp.concatenate([block(kind, j).astype(F32) for block in blocks], axis=0)
            start = j * width + kind * C
            table[:, start : start + C] = column.astype(BF16)


def source_hot(ids, atoms):
    place = ids ^ (lax.axis_index("row") * 8)
    return place == iota((atoms, ids.shape[1]), 0)


def target_hot(ids, atoms):
    place = ids ^ (lax.axis_index("col") * 8)
    block = place // 8
    outer = atoms // (8 * INNER)
    place = ((block % INNER) * outer + block // INNER) * 8 + place % 8
    return place == iota((atoms, ids.shape[1]), 0)


def store_pair(packed, slot, first, second):
    groups = packed.shape[0]
    first = first.reshape(groups, GROUP, -1)
    second = second.reshape(groups, GROUP, -1)
    rows = slice(slot * GROUP, slot * GROUP + 2 * GROUP)
    packed[:, rows, :] = jnp.concatenate([first, second], axis=1).astype(BF16)


def clear_rows(packed, slots):
    groups, rows, width = packed.shape
    for g in range(groups):
        packed[g, slots * GROUP :, :] = jnp.zeros((rows - slots * GROUP, width), packed.dtype)


def gather_atoms(hot, table, packed):
    hot = jnp.where(hot, 1.0, 0.0).T.astype(BF16)
    width = packed.shape[2]
    for j in range(0, COEF, 2):
        count = min(2, COEF - j)
        value = jnp.dot(
            hot, table[:, j * width : (j + count) * width], preferred_element_type=F32
        )
        first = value[:, :width]
        second = value[:, width:] if count == 2 else jnp.zeros_like(first)
        store_pair(packed, j, first, second)


def rotate_group(rot_ref, g, packed, local_g):
    return jnp.dot(rot_ref[g], packed[local_g], preferred_element_type=F32)


def pair_row(first, second, k, kind=0):
    lanes = slice(kind * C, (kind + 1) * C)
    return jnp.concatenate([first[k * 8 : k * 8 + 8, lanes], second[k * 8 : k * 8 + 8, lanes]], 0)


def store_forward(value, lefts, top, low):
    for k in range(5):
        lefts[0][top, k * C : (k + 1) * C] = value(k).astype(BF16)
    for left, base, count in ((lefts[1], 5, 4), (lefts[2], 13, 3)):
        for n in range(count):
            p, q = value(base + n), value(base + count + n)
            here = slice(n * C, (n + 1) * C)
            there = slice((count + n) * C, (count + n + 1) * C)
            left[top, here] = p.astype(BF16)
            left[top, there] = (-q).astype(BF16)
            left[low, here] = q.astype(BF16)
            left[low, there] = p.astype(BF16)


def half_weight(w_ref, n, half):
    width = w_ref.shape[-1]
    if n == 0:
        return w_ref[:, half].reshape(-1, width)
    return w_ref[:, :, half].reshape(-1, width)


def source_forward_kernel(count_pieces, *refs):
    ids_ref, rot_ref = refs[:2]
    w_refs, pieces = refs[2:5], refs[5 : 5 + count_pieces]
    refs = refs[5 + count_pieces :]
    outs, table, packed, lefts = refs[:3], refs[3], refs[4], refs[5:]
    edges = ids_ref.shape[1]
    blocks = [lambda kind, j, piece=piece: piece[j] for piece in pieces]
    fill_table(blocks, table, 1)
    clear_rows(packed, COEF + 1)

    gather_atoms(source_hot(ids_ref[...], table.shape[0]), table, packed)
    for g in range(0, edges // GROUP, 2):
        pair = [rotate_group(rot_ref, g + n, packed, g + n) for n in range(2)]
        top, low = slice(g * 8, g * 8 + 16), slice(edges + g * 8, edges + g * 8 + 16)
        store_forward(lambda k: pair_row(*pair, k), lefts, top, low)
    for n in range(3):
        outs[n][...] = jnp.dot(
            lefts[n][...], half_weight(w_refs[n], n, 0), preferred_element_type=F32
        )


def y_slices(start):
    out = [(0, start, k) for k in range(5)]
    for which, count in ((1, 4), (2, 3)):
        for sign in range(2):
            out += [(which, start + sign * CHUNK, n) for n in range(count)]
    return out


def back_half(half, first, lefts, w_refs, rot_ref, packed, edge_grad):
    groups = packed.shape[0]
    count = groups * GROUP
    edges = lefts[0].shape[0]
    for n, terms, slot in ((0, 5, 0), (1, 4, 6), (2, 3, 14)):
        width = w_refs[n].shape[-1]
        for k in range(0, terms, 2):
            until = min(k + 2, terms)
            for sign in range(1 if n == 0 else 2):
                here = pl.ds(aligned(first + sign * edges, GROUP), count)
                if n == 0:
                    weight = w_refs[n][k:until, half].reshape(-1, width)
                    value = lax.dot_general(
                        lefts[n][here, :], weight, NT, preferred_element_type=F32
                    )
                else:
                    real = w_refs[n][0, k:until, half].reshape(-1, width)
                    imag = w_refs[n][1, k:until, half].reshape(-1, width)
                    value = lax.dot_general(
                        lefts[n][here, :width], real, NT, preferred_element_type=F32
                    ) + lax.dot_general(
                        lefts[n][here, width:], imag, NT, preferred_element_type=F32
                    )
                one = value[:, :C]
                two = value[:, C:] if until - k == 2 else jnp.zeros_like(one)
                store_pair(packed, slot + sign * (terms + 1) // 2 * 2 + k, one, two)

    at = first // GROUP
    for g in range(0, groups, 2):
        pair = [rotate_group(rot_ref, at + g + n, packed, g + n) for n in range(2)]
        rows = pl.ds(aligned(first + g * 8, 16), 16)
        for j in range(COEF):
            edge_grad[rows, j * C : (j + 1) * C] = pair_row(*pair, j).astype(BF16)


def scatter_atoms(hot, count_ref, edge_grad, out_ref):
    valid = iota(hot.shape, 1) < count_ref[0, 0]
    hot = jnp.where(hot & valid, 1.0, 0.0).astype(BF16)
    for j in range(0, COEF, 2):
        until = min(j + 2, COEF)
        total = jnp.dot(hot, edge_grad[:, j * C : until * C], preferred_element_type=F32)
        for n in range(until - j):
            for b in range(out_ref.shape[0]):
                block = total[b * 8 : b * 8 + 8, n * C : (n + 1) * C]
                out_ref[b, j + n] = block.astype(out_ref.dtype)


def target_kernel(count_pieces, *refs):
    ids_ref, count_ref, fwd_ref, bwd_ref = refs[:4]
    w_refs, sources = refs[4:7], refs[7:10]
    pieces = refs[10 : 10 + count_pieces]
    refs = refs[10 + count_pieces :]
    lefts, out_ref = refs[:3], refs[3]
    table, packed = refs[4], refs[5]
    forward_lefts, cots, ys, packed_back = refs[6:9], refs[9], refs[10:13], refs[13]
    edge_grad = refs[14]
    edges = ids_ref.shape[1]
    blocks = []
    for piece in pieces:
        for b in range(piece.shape[0]):
            blocks.append(lambda kind, j, piece=piece, b=b: piece[b, kind, j])
    fill_table(blocks, table, 2)
    clear_rows(packed, COEF + 1)
    clear_rows(packed_back, len(SLOTS))

    def chunk_step(chunk, unused):
        first = aligned(chunk * CHUNK, CHUNK)
        hot = target_hot(ids_ref[:, pl.ds(first, CHUNK)], table.shape[0])
        gather_atoms(hot, table, packed)

        for g in range(0, CHUNK // GROUP, 2):
            at = chunk * (CHUNK // GROUP) + g
            pair = [rotate_group(fwd_ref, at + n, packed, g + n) for n in range(2)]
            top, low = slice(g * 8, g * 8 + 16), slice(CHUNK + g * 8, CHUNK + g * 8 + 16)
            store_forward(lambda k: pair_row(*pair, k), forward_lefts, top, low)
            for k in range(ROWS):
                cots[top, k * C : (k + 1) * C] = pair_row(*pair, k, 1).astype(BF16)
        for n in range(3):
            value = jnp.dot(
                forward_lefts[n][...], half_weight(w_refs[n], n, 1), preferred_element_type=F32
            )
            for sign in range(1 if n == 0 else 2):
                here = slice(sign * CHUNK, (sign + 1) * CHUNK)
                there = pl.ds(aligned(first + sign * edges, CHUNK), CHUNK)
                ys[n][here, :] = sources[n][there, :] + value[here]

        def gate(i, unused):
            start = aligned(i * 16, 16)
            top = pl.ds(start, 16)
            cot = [cots[top, k * C : (k + 1) * C].astype(F32) for k in range(ROWS)]
            where = y_slices(start)

            def y_at(k):
                which, row, n = where[k]
                return ys[which][pl.ds(aligned(row, 16), 16), n * C : (n + 1) * C]

            y0 = y_at(0)
            gating = jax.nn.sigmoid(y0)
            slope = gating * (1.0 - gating)
            dotted = cot[1] * y_at(1)
            for k in range(2, ROWS):
                dotted = dotted + cot[k] * y_at(k)
            grads = [cot[0] * (gating + y0 * slope) + dotted * slope]
            grads += [gating * cot[k] for k in range(1, ROWS)]
            store_backward(grads, lefts, first + start)
            return unused

        lax.fori_loop(0, CHUNK // 16, gate, 0, unroll=True)
        back_half(1, first, lefts, w_refs, bwd_ref, packed_back, edge_grad)
        return unused

    lax.fori_loop(0, edges // CHUNK, chunk_step, 0, unroll=True)
    scatter_atoms(target_hot(ids_ref[...], table.shape[0]), count_ref, edge_grad, out_ref)


def store_backward(value, lefts, row):
    top = pl.ds(aligned(row, 16), 16)
    low = pl.ds(aligned(row + lefts[0].shape[0], 16), 16)
    for k in range(5):
        lefts[0][top, k * C : (k + 1) * C] = value[k].astype(BF16)
    for left, base, count in ((lefts[1], 5, 4), (lefts[2], 13, 3)):
        for n in range(count):
            a, b = value[base + n], value[base + count + n]
            here = slice(n * C, (n + 1) * C)
            there = slice((count + n) * C, (count + n + 1) * C)
            left[top, here] = a.astype(BF16)
            left[top, there] = b.astype(BF16)
            left[low, here] = b.astype(BF16)
            left[low, there] = (-a).astype(BF16)


def source_back_kernel(*refs):
    ids_ref, count_ref, bwd_ref = refs[:3]
    w_refs, lefts, out_ref = refs[3:6], refs[6:9], refs[9]
    packed, edge_grad = refs[10:]
    clear_rows(packed, len(SLOTS))
    back_half(0, 0, lefts, w_refs, bwd_ref, packed, edge_grad)
    scatter_atoms(source_hot(ids_ref[...], out_ref.shape[0] * 8), count_ref, edge_grad, out_ref)


IN_VMEM = pl.BlockSpec(memory_space=pltpu.VMEM)
IN_SMEM = pl.BlockSpec(memory_space=pltpu.SMEM)


def call(kernel, args, outs, scratch, limit, flops, scalar=None):
    moved = sum(a.size * a.dtype.itemsize for a in (*args, *outs))
    return pl.pallas_call(
        kernel,
        in_specs=[IN_SMEM if n == scalar else IN_VMEM for n in range(len(args))],
        out_specs=[IN_VMEM] * len(outs),
        out_shape=outs,
        scratch_shapes=[pltpu.VMEM(s, d) for s, d in scratch],
        compiler_params=pltpu.CompilerParams(vmem_limit_bytes=limit * MIB),
        cost_estimate=pl.CostEstimate(flops=flops, bytes_accessed=moved, transcendentals=0),
    )(*args)


def arrays(shapes, dtype):
    return [jax.ShapeDtypeStruct(s, dtype) for s in shapes]


def y_shapes(edges):
    return [(edges, 5 * C), (2 * edges, 4 * C), (2 * edges, 3 * C)]


def left_shapes(edges):
    return [(edges, 5 * C), (2 * edges, 8 * C), (2 * edges, 6 * C)]


def typed(shapes, dtype):
    return [(s, dtype) for s in shapes]


def packed_shape(edges, kinds):
    return (edges // GROUP, LANES, kinds * C)


PUSH = 2 * 65536


def expand_fwd(tall):
    edges = tall.shape[1]
    outs = arrays([(edges // GROUP, K_PAD, LANES), (edges, 512)], BF16)
    scratch = [((512, edges), F32)]
    return call(expand_fwd_kernel, [tall], outs, scratch, 6, PUSH * edges * 20)


def expand_bwd(flat):
    edges = flat.shape[0]
    outs = arrays([(edges // GROUP, J_PAD, LANES)], BF16)
    return call(expand_bwd_kernel, [flat], outs, [((edges, 512), BF16)], 6, PUSH * edges * 30)[0]


def source_forward(ids, pieces, rot, weights):
    edges = ids.shape[1]
    scratch = [((len(pieces) * 8, COEF * C), BF16), (packed_shape(edges, 1), BF16)]
    scratch += typed(left_shapes(edges), BF16)
    return call(
        functools.partial(source_forward_kernel, len(pieces)),
        [ids, rot, *weights, *pieces],
        arrays(y_shapes(edges), F32),
        scratch,
        14,
        PUSH * edges * 64,
    )


def target_work(ids, count, fwd, bwd, weights, sources, pieces):
    edges = ids.shape[1]
    blocks = sum(p.shape[0] for p in pieces)
    outs = arrays(left_shapes(edges), BF16) + arrays([(blocks, COEF, 8, C)], BF16)
    scratch = [((blocks * 8, 2 * COEF * C), BF16), (packed_shape(CHUNK, 2), BF16)]
    scratch += typed(left_shapes(CHUNK), BF16) + [((CHUNK, ROWS * C), BF16)]
    scratch += typed(y_shapes(CHUNK), F32) + [(packed_shape(CHUNK, 1), BF16)]
    scratch += [((edges, COEF * C), BF16)]
    return call(
        functools.partial(target_kernel, len(pieces)),
        [ids, count, fwd, bwd, *weights, *sources, *pieces],
        outs,
        scratch,
        21 + blocks // 4,
        PUSH * edges * 160,
        1,
    )


def source_back(ids, count, bwd, weights, lefts, blocks):
    edges = lefts[0].shape[0]
    scratch = [(packed_shape(edges, 1), BF16), ((edges, COEF * C), BF16)]
    return call(
        source_back_kernel,
        [ids, count, bwd, *weights, *lefts],
        arrays([(blocks, COEF, 8, C)], BF16),
        scratch,
        12,
        PUSH * edges * 70,
        1,
    )[0]


def exchange(value, axis, distance):
    size = lax.axis_size(axis)
    return lax.ppermute(value, axis, [(i, i ^ distance) for i in range(size)])


def step(node_feats, grad_out, edge_src, edge_tgt, count, wigner, w_zero, w_one, w_two):
    rows, cols = lax.axis_size("row"), lax.axis_size("col")
    inner, outer = INNER, cols // INNER
    feats = node_feats.transpose(1, 0, 2)
    own = jnp.stack([feats, grad_out.transpose(1, 0, 2)])
    line = []
    for d in range(1, outer):
        line.append(exchange(own, "col", inner * d))
    own_first = exchange(own, "col", 1)
    own_second = exchange(own, "col", 2)
    source_feats = [feats] + [exchange(feats, "row", d) for d in range(1, rows)]
    line = jnp.stack(line)
    first = exchange(line, "col", 1)
    second = exchange(line, "col", 2)
    cut = outer // 2
    far_first = exchange(first[:cut], "col", 2)
    rest = jnp.concatenate([own_second[None], second[cut:]])
    far_second = exchange(rest, "col", 1)
    pieces = [own[None], line, own_first[None], first, own_second[None], second]
    pieces += [far_second[:1], far_first, far_second[1:]]

    weights = (
        w_zero.reshape(5, 2, C, 5 * C),
        w_one.reshape(2, 4, 2, C, 4 * C),
        w_two.reshape(2, 3, 2, C, 3 * C),
    )
    edges = edge_src.shape[-1]
    src, tgt = edge_src.reshape(1, edges), edge_tgt.reshape(1, edges)
    fwd, flat = expand_fwd(wigner[0, 0].T)
    bwd = expand_bwd(flat)
    sources = source_forward(src, source_feats, fwd, weights)
    *lefts, tile_tgt = target_work(tgt, count, fwd, bwd, weights, sources, pieces)
    tile_src = source_back(src, count, bwd, weights, lefts, rows)

    parts = tile_tgt.reshape(inner, outer, COEF, 8, C)
    summed = parts[0].astype(F32)
    for d in range(1, inner):
        got = exchange(parts[d], "col", d)
        summed = summed + got.astype(F32)
    sent = summed.astype(BF16)
    result = summed[0]
    for d in range(1, outer):
        got = exchange(sent[d], "col", inner * d)
        result = result + got.astype(F32)
    result = result + tile_src[0].astype(F32)
    for d in range(1, rows):
        result = result + exchange(tile_src[d], "row", d).astype(F32)
    return result.transpose(1, 0, 2)


def solution(mesh):
    placed = (
        P(("row", "col"), None, None),
        P(("row", "col"), None, None),
        P("row", "col", None),
        P("row", "col", None),
        P("row", "col"),
        P("row", "col", None, None),
        P(),
        P(),
        P(),
    )
    return jax.shard_map(
        step, mesh=mesh, in_specs=placed, out_specs=P(("row", "col"), None, None), check_vma=False
    )
```
